256 devices in a mesh: depth: 32 (over x, z), views: 8 (over y, core).
Axes of the slice: x: 4, y: 4, z: 8, core: 2. Of those that a mesh axis runs over, the one named last changes fastest.
Arguments:
- density: bfloat16 [512, 128, 128], P('depth'), may hold values from 0.25 to 4
- row_index: int32 [16, 192], replicated, may hold values from 0 to 126, as said below
- row_weight: float32 [16, 192], replicated, may hold values from 0 to 1
- col_index: int32 [16, 192], replicated, may hold values from 0 to 126, as said below
- col_weight: float32 [16, 192], replicated, may hold values from 0 to 1
- assignment: int32 [16], P('views'), may hold values from 0 to 15, each once
- target_image: float32 [16, 36864], P('views'), may hold values from 0.4 to 2
Outputs:
- rendered: float32 [16, 36864], P('views')
- voxel_grad: float32 [512, 128, 128], P(('depth', 'views'))
The draws below stay inside these ranges and needn't reach their ends.
Inputs may be any that keep to these rules, and one draw needn't show every extreme that they name: `row_index`: along the pixels of each view the indices never fall. `col_index`: along the pixels of each view the indices never fall. `assignment`: each of the 16 views appears once.
All inputs are finite; a program needn't handle non-finite values.
Results may differ from the reference program's by a relative error of at most 0.0046.
Values sent between devices are 32-bit elements; how exact they have to be, the bound alone decides.
A program may use at most 192 MiB of HBM per device.

```python
import math
import jax
import jax.numpy as jnp
from jax import lax

A = 128
P_SIZE = 192
ALLV = 16
NZ = 512


def index_table(key, salt):
    key = jax.random.fold_in(key, salt)
    first_key, second_key, third_key = jax.random.split(key, 3)
    lowest = jax.random.randint(first_key, (ALLV,), 0, A // 4 + 1)
    highest = jax.random.randint(second_key, (ALLV,), 3 * A // 4, A - 1)
    picked = jax.random.randint(third_key, (), 0, ALLV)
    numbers = jnp.arange(ALLV)
    lowest = jnp.where(numbers == picked, 0, lowest)
    highest = jnp.where(numbers == (picked + 1) % ALLV, A - 2, highest)
    steps = jnp.arange(P_SIZE)
    table = lowest[:, None] + steps[None, :] * (highest - lowest)[:, None] // (P_SIZE - 1)
    return table.astype(jnp.int32)


def draw_row_index(key, part):
    return index_table(key, 101)


def draw_col_index(key, part):
    return index_table(key, 202)


def shard_levels(rng, shape, cuts, low, largest):
    gain, own = 1.0, jax.random.fold_in(rng, 6)
    for axis_at, blocks in cuts:
        heights = jnp.exp(jax.random.uniform(jax.random.fold_in(own, axis_at), (blocks,), jnp.float32, low / len(cuts), largest / len(cuts)))
        gain = gain * jnp.repeat(heights, shape[axis_at] // blocks).reshape([-1 if axis == axis_at else 1 for axis in range(len(shape))])
    return gain


def setup_inputs(seed: int = 0) -> dict:
    streams_of = jax.random.split(jax.random.key(seed), 8)
    density = jnp.clip(jnp.exp(math.log(4.0) - 2.7725887 * jax.random.uniform(streams_of[0], (NZ, A, A), jnp.float32) ** shard_levels(streams_of[0], (NZ, A, A), ((0, 32),), -0.2, 0.2)), 0.25, 4.0).astype(jnp.bfloat16)
    row_index = draw_row_index(jax.random.fold_in(streams_of[7], 71), 0)
    row_weight = jnp.clip(jax.random.uniform(streams_of[2], (ALLV, P_SIZE), jnp.float32, 0.0, 1.0), 0.0, 1.0)
    col_index = draw_col_index(jax.random.fold_in(streams_of[7], 71), 0)
    col_weight = jnp.clip(jax.random.uniform(streams_of[4], (ALLV, P_SIZE), jnp.float32, 0.0, 1.0), 0.0, 1.0)
    assignment = jax.random.permutation(streams_of[5], ALLV).astype(jnp.int32)
    target_image = jnp.clip(0.4 + 1.6 * jax.random.uniform(streams_of[6], (ALLV, P_SIZE * P_SIZE), jnp.float32) ** shard_levels(streams_of[6], (ALLV, P_SIZE * P_SIZE), ((0, 8),), -0.2, 0.2), 0.4, 2.0)
    return dict(density=density, row_index=row_index, row_weight=row_weight, col_index=col_index, col_weight=col_weight, assignment=assignment, target_image=target_image)


def rounded(values):
    return lax.optimization_barrier(values.astype(jnp.bfloat16)).astype(jnp.float32)


def resampler(indices, weights, cells):
    places = lax.broadcasted_iota(jnp.int32, indices.shape + (cells,), indices.ndim)
    lower = (places == indices[..., None]).astype(jnp.float32)
    upper = (places == indices[..., None] + 1).astype(jnp.float32)
    return rounded((1.0 - weights[..., None]) * lower + weights[..., None] * upper)


def reference(density, row_index, row_weight, col_index, col_weight, assignment, target_image):
    levels = density.shape[0]
    cells = density.shape[1]
    pixels = row_index.shape[1]
    step_scale = 1.5 / levels
    dense_vol = density.astype(jnp.float32)

    def render(carry, which_slot):
        view = assignment[which_slot]
        rows_matrix = resampler(row_index[view], row_weight[view], cells)
        cols_matrix = resampler(col_index[view], col_weight[view], cells)
        partial_rows = rounded(jnp.einsum("ia,zab->zib", rows_matrix, dense_vol))
        samples = jnp.einsum("zib,jb->zij", partial_rows, cols_matrix).reshape(levels, pixels * pixels)
        optical = step_scale * samples
        attenuate = jnp.exp(-optical)
        emitted = samples * (1.0 - attenuate)
        running = jnp.cumsum(optical, axis=0)
        through = jnp.exp(-(running - optical))
        inclusive = jnp.cumsum(through * emitted, axis=0)
        image = inclusive[-1]
        residue = image - target_image[which_slot]
        grad_samples = levels * residue[None, :] * (through * ((1.0 - attenuate) + optical * attenuate) - step_scale * (image[None, :] - inclusive))
        grad_samples = rounded(grad_samples).reshape(levels, pixels, pixels)
        spread = rounded(jnp.einsum("zij,jb->zib", grad_samples, cols_matrix))
        return carry + jnp.einsum("ia,zib->zab", rows_matrix, spread), image

    start_grad = jnp.zeros((levels, cells, cells), jnp.float32)
    voxel_grad, images = lax.scan(render, start_grad, jnp.arange(ALLV).astype(jnp.int32))
    return images, voxel_grad
```

```python
import functools

import jax
import jax.numpy as jnp
from jax import lax
from jax.experimental import pallas as pl
from jax.experimental.pallas import tpu as pltpu
from jax.sharding import PartitionSpec as P

MESH = pl.DeviceIdType.MESH
ZDEV = 8
BF = jnp.bfloat16
F32 = jnp.float32


def spread_order(n):
    out = []
    for k in range(1, n // 2 + 1):
        for o in (k, n - k):
            if o not in out and 0 < o < n:
                out.append(o)
    return out


def kernel(
    dims, assign, density, row_index, row_weight, col_index, col_weight, target, image, grad,
    pad_i, pad_w, tall, rows_m, rows_t, cols_m, cols_t, work, goal, gain, shift,
    mine, theirs, local, slab, slabs, back, final, give, got, keep, summed, pieces,
    s1, r1, s2, r2, s3, r3, s4, r4, s5, r5,
):
    nx, nz, ny, levels = dims
    step = 1.5 / levels
    slices, cells = density.shape[0], density.shape[1]
    half = row_index.shape[1] // 2
    pixels = 2 * half
    wide = 2 * pixels
    chunks = 2 * half // 8 // nz
    share = slices // (2 * ny)
    depth, vw = lax.axis_index("depth"), lax.axis_index("views")
    x, z = depth // nz, depth % nz
    y, core = vw // 2, vw % 2

    def at_z(q):
        return (x * nz + q, vw)

    def at_x(q):
        return (q * nz + z, vw)

    def at_y(q):
        return (depth, q * 2 + core)

    partner = (depth, y * 2 + 1 - core)
    z_off, x_off, y_off = spread_order(nz), spread_order(nx), spread_order(ny)

    barrier = pltpu.get_barrier_semaphore()
    for o in z_off:
        pl.semaphore_signal(barrier, inc=1, device_id=at_z((z + o) % nz), device_id_type=MESH)
    for o in x_off:
        pl.semaphore_signal(barrier, inc=1, device_id=at_x((x + o) % nx), device_id_type=MESH)
    for o in y_off:
        pl.semaphore_signal(barrier, inc=1, device_id=at_y((y + o) % ny), device_id_type=MESH)
    pl.semaphore_signal(barrier, inc=1, device_id=partner, device_id_type=MESH)

    pad_i[...] = jnp.full(pad_i.shape, -2, jnp.int32)
    pad_w[...] = jnp.zeros(pad_w.shape, F32)
    for v in range(2):
        a = assign[v]
        pad_i[v : v + 1, 0:pixels] = row_index[pl.ds(a, 1), :]
        pad_w[v : v + 1, 0:pixels] = row_weight[pl.ds(a, 1), :]
        pad_i[2 + v : 3 + v, 0:pixels] = col_index[pl.ds(a, 1), :]
        pad_w[2 + v : 3 + v, 0:pixels] = col_weight[pl.ds(a, 1), :]

    def resampler(row, lanes):
        idx, w = pad_i[row : row + 1, 0:lanes], pad_w[row : row + 1, 0:lanes]
        places = lax.broadcasted_iota(jnp.int32, (cells, lanes), 0)
        zero = jnp.zeros((cells, lanes), F32)
        return jnp.where(places == idx, 1.0 - w, zero) + jnp.where(places == idx + 1, w, zero)

    for v in range(2):
        tall[v] = resampler(v, 2 * cells).T
        ct = resampler(2 + v, wide)
        both = jnp.concatenate([ct, pltpu.roll(ct, pixels, 1)], axis=0)
        cols_m[v] = both.astype(BF)
        cols_t[v] = both.T.astype(BF)
    rows = jnp.concatenate(
        [tall[v, pl.ds(p, half, stride=2), :] for p in range(2) for v in range(2)], axis=0
    )
    rows_m[...] = rows.astype(BF)
    rows_t[...] = rows.T.astype(BF)

    def sample(pair, carry):
        two = jnp.concatenate([density[2 * pair], density[2 * pair + 1]], axis=1)
        part = jnp.dot(rows_m[...], two, preferred_element_type=F32).astype(BF)
        for v in range(2):
            lhs = jnp.concatenate(
                [
                    jnp.concatenate(
                        [
                            part[(2 * p + v) * half : (2 * p + v + 1) * half, s * cells : (s + 1) * cells]
                            for p in range(2)
                        ],
                        axis=1,
                    )
                    for s in range(2)
                ],
                axis=0,
            )
            out = jnp.dot(lhs, cols_m[v], preferred_element_type=F32)
            for s in range(2):
                work[2 * pair + s, v * half : (v + 1) * half, :] = out[s * half : (s + 1) * half]
        return carry

    lax.fori_loop(0, slices // 2, sample, 0)

    def march(tile, carry):
        at = pl.ds(pl.multiple_of(tile * 8, 8), 8)
        through = jnp.ones((8, wide), F32)
        inclusive = jnp.zeros((8, wide), F32)
        for s in range(slices):
            value = work[s, at, :]
            optical = step * value
            att = jnp.exp(-optical)
            gone = 1.0 - att
            inclusive = inclusive + through * (value * gone)
            work[s, at, :] = through * (gone + optical * att) + step * inclusive
            through = through * att
        mine[tile, 0] = inclusive
        mine[tile, 1] = through
        return carry

    pending = []

    def send(src, dst, ssem, rsem, device):
        copy = pltpu.make_async_remote_copy(
            src_ref=src, dst_ref=dst, send_sem=ssem, recv_sem=rsem, device_id=device, device_id_type=MESH
        )
        copy.start()
        pending.append(copy)

    def arrived(dst, rsem):
        pltpu.make_async_remote_copy(
            src_ref=dst, dst_ref=dst, send_sem=rsem, recv_sem=rsem, device_id=partner, device_id_type=MESH
        ).wait_recv()

    for k in range(chunks):
        lax.fori_loop(k * nz, (k + 1) * nz, march, 0)
        if k == 0:
            pl.semaphore_wait(barrier, len(z_off) + len(x_off) + len(y_off) + 1)
        for o in z_off:
            q = (z + o) % nz
            send(mine.at[k * nz + q], theirs.at[k, z], s1.at[k, q], r1.at[k, z], at_z(q))

    for v in range(2):
        for g in range(wide // 128):
            goal[v * half : (v + 1) * half, g * 128 : (g + 1) * 128] = target[
                pl.ds(2 * g + v, half, stride=2 * wide // 128), :
            ]

    def slab_of(k):
        theirs[k, z] = mine[k * nz + z]
        for o in z_off:
            q = (z + o) % nz
            arrived(theirs.at[k, q], r1.at[k, q])
        c = jnp.zeros((8, wide), F32)
        t = jnp.ones((8, wide), F32)
        for q in range(nz):
            local[k, q, 0] = c
            local[k, q, 1] = t
            c = c + t * theirs[k, q, 0]
            t = t * theirs[k, q, 1]
        slab[k, 0] = c
        slab[k, 1] = t
        slabs[k, x, 0] = c
        slabs[k, x, 1] = t
        for o in x_off:
            q = (x + o) % nx
            send(slab.at[k], slabs.at[k, x], s2.at[k, q], r2.at[k, x], at_x(q))

    def lead_of(k):
        for o in x_off:
            q = (x + o) % nx
            arrived(slabs.at[k, q], r2.at[k, q])
        lead_c = jnp.zeros((8, wide), F32)
        lead_t = jnp.ones((8, wide), F32)
        c, t = lead_c, lead_t
        for q in range(nx):
            c = c + t * slabs[k, q, 0]
            t = t * slabs[k, q, 1]
            earlier = q < x
            lead_c = jnp.where(earlier, c, lead_c)
            lead_t = jnp.where(earlier, t, lead_t)
        for q in range(nz):
            back[k, q, 0] = lead_t * local[k, q, 1]
            back[k, q, 1] = c - (lead_c + lead_t * local[k, q, 0])
            back[k, q, 2] = c
        for o in z_off:
            q = (z + o) % nz
            send(back.at[k, q], final.at[k * nz + z], s3.at[k, q], r3.at[k, z], at_z(q))
        final[k * nz + z] = back[k, z]

    for k in range(chunks + 1):
        if k < chunks:
            slab_of(k)
        if k >= 1:
            lead_of(k - 1)

    for k in range(chunks):
        for o in z_off:
            q = (z + o) % nz
            arrived(final.at[k * nz + q], r3.at[k, q])
    per = half // 8
    for v in range(2):
        at = slice(v * half, (v + 1) * half)
        residue = levels * (final[v * per : (v + 1) * per, 2].reshape(half, wide) - goal[at])
        gain[at] = residue * final[v * per : (v + 1) * per, 0].reshape(half, wide)
        shift[at] = step * residue * final[v * per : (v + 1) * per, 1].reshape(half, wide)

    def terms(first):
        g = [(gain[...] * work[first + s] - shift[...]).astype(BF) for s in range(2)]
        spread = [
            jnp.dot(
                jnp.concatenate([g[s][v * half : (v + 1) * half] for s in range(2)], axis=0),
                cols_t[v],
                preferred_element_type=F32,
            ).astype(BF)
            for v in range(2)
        ]
        stack = jnp.concatenate(
            [
                jnp.concatenate(
                    [
                        spread[v][s * half : (s + 1) * half, p * cells : (p + 1) * cells]
                        for p in range(2)
                        for v in range(2)
                    ],
                    axis=0,
                )
                for s in range(2)
            ],
            axis=1,
        )
        out = jnp.dot(rows_t[...], stack, preferred_element_type=F32)
        return [out[:, s * cells : (s + 1) * cells] for s in range(2)]

    def merge(o):
        q = (y + o) % ny
        arrived(got.at[q], r4.at[q])
        summed[q] = keep[q] + got[q]
        if o:
            send(summed.at[q], pieces.at[y], s5.at[q], r5.at[y], at_y(q))

    order = y_off[::-1] + [0]
    for n, o in enumerate(order):
        q = (y + o) % ny
        for i in range(0, share, 2):
            out = terms((2 * q + 1 - core) * share + i)
            for s in range(2):
                give[q, i + s] = out[s]
        send(give.at[q], got.at[q], s4.at[q], r4.at[q], partner)
        for i in range(0, share, 2):
            out = terms((2 * q + core) * share + i)
            for s in range(2):
                keep[q, i + s] = out[s]
        if n:
            merge(order[n - 1])
    merge(0)

    for v in range(2):
        for g in range(wide // 128):
            image[pl.ds(2 * g + v, half, stride=2 * wide // 128), :] = final[
                v * per : (v + 1) * per, 2, :, g * 128 : (g + 1) * 128
            ].reshape(half, 128)

    total = summed[y]
    for o in y_off:
        q = (y + o) % ny
        arrived(pieces.at[q], r5.at[q])
        total = total + pieces[q]
    grad[...] = total
    for copy in pending:
        copy.wait_send()


def on_device(nx, nz, ny, density, row_index, row_weight, col_index, col_weight, assignment, target_image):
    slices, cells = density.shape[0], density.shape[1]
    views, flat = target_image.shape
    pixels = row_index.shape[1]
    wide, tiles = 2 * pixels, flat * views // (8 * 2 * pixels)
    chunks = tiles // nz
    share = slices // (2 * ny)
    lines = flat // 128
    vm = pl.BlockSpec(memory_space=pltpu.VMEM)
    dma = pltpu.SemaphoreType.DMA
    image, grad = pl.pallas_call(
        functools.partial(kernel, (nx, nz, ny, slices * nx * nz)),
        out_shape=(
            jax.ShapeDtypeStruct((views * lines, 128), F32),
            jax.ShapeDtypeStruct((share, cells, cells), F32),
        ),
        in_specs=[pl.BlockSpec(memory_space=pltpu.SMEM)] + [vm] * 6,
        out_specs=(vm, vm),
        scratch_shapes=[
            pltpu.VMEM((8, wide), jnp.int32),
            pltpu.VMEM((8, wide), F32),
            pltpu.VMEM((2, 2 * cells, cells), F32),
            pltpu.VMEM((wide, cells), BF),
            pltpu.VMEM((cells, wide), BF),
            pltpu.VMEM((2, 2 * cells, wide), BF),
            pltpu.VMEM((2, wide, 2 * cells), BF),
            pltpu.VMEM((slices, pixels, wide), F32),
            pltpu.VMEM((pixels, wide), F32),
            pltpu.VMEM((pixels, wide), F32),
            pltpu.VMEM((pixels, wide), F32),
            pltpu.VMEM((tiles, 2, 8, wide), F32),
            pltpu.VMEM((chunks, nz, 2, 8, wide), F32),
            pltpu.VMEM((chunks, nz, 2, 8, wide), F32),
            pltpu.VMEM((chunks, 2, 8, wide), F32),
            pltpu.VMEM((chunks, nx, 2, 8, wide), F32),
            pltpu.VMEM((chunks, nz, 3, 8, wide), F32),
            pltpu.VMEM((tiles, 3, 8, wide), F32),
            pltpu.VMEM((ny, share, cells, cells), F32),
            pltpu.VMEM((ny, share, cells, cells), F32),
            pltpu.VMEM((ny, share, cells, cells), F32),
            pltpu.VMEM((ny, share, cells, cells), F32),
            pltpu.VMEM((ny, share, cells, cells), F32),
            dma((chunks, nz)), dma((chunks, nz)),
            dma((chunks, nx)), dma((chunks, nx)),
            dma((chunks, nz)), dma((chunks, nz)),
            dma((ny,)), dma((ny,)),
            dma((ny,)), dma((ny,)),
        ],
        compiler_params=pltpu.CompilerParams(
            collective_id=0, has_side_effects=True, vmem_limit_bytes=48 << 20
        ),
    )(
        assignment, density, row_index, row_weight, col_index, col_weight,
        target_image.reshape(views, lines, 128).transpose(1, 0, 2).reshape(views * lines, 128),
    )
    return image.reshape(lines, views, 128).transpose(1, 0, 2).reshape(views, flat), grad


def solution(mesh, nz=ZDEV):
    placed = (P("depth", None, None), P(), P(), P(), P(), P("views"), P("views", None))
    nx, ny = mesh.shape["depth"] // nz, mesh.shape["views"] // 2
    return jax.shard_map(
        functools.partial(on_device, nx, nz, ny),
        mesh=mesh,
        in_specs=placed,
        out_specs=(P("views", None), P(("depth", "views"), None, None)),
        check_vma=False,
    )
```

```python
import functools

import jax
import jax.numpy as jnp
from jax import lax
from jax.experimental import pallas as pl
from jax.experimental.pallas import tpu as pltpu
from jax.sharding import PartitionSpec as P

MESH = pl.DeviceIdType.MESH
ZDEV = 8
BF = jnp.bfloat16
F32 = jnp.float32
LOG2E = 1.4426950408889634


def spread_order(n):
    out = []
    for k in range(1, n // 2 + 1):
        for o in (k, n - k):
            if o not in out and 0 < o < n:
                out.append(o)
    return out


def kernel(
    dims, *refs
):
    (
    assign_h, density_h, row_index_h, row_weight_h, col_index_h, col_weight_h, target_h, image, grad,
    assign, density, row_index, row_weight, col_index, col_weight, target, loads,
    pad_i, pad_w, tall, rows_m, rows_t, cols_m, cols_t, crossed, work, goal, gain, shift,
    mine, theirs, local, slab, slabs, back, final, totals, part, give, got, keep, summed, pieces,
    s1, r1, s2, r2, s3, r3, s4, r4, s5, r5, s6, r6, s7, r7,
    ) = refs
    nx, nz, ny, levels = dims
    step = 1.5 / levels
    slices, cells = density.shape[0], density.shape[1]
    half = row_index.shape[1] // 2
    pixels = 2 * half
    wide = 2 * pixels
    chunks = 2 * half // 8 // nz
    share = slices // (2 * ny)
    depth, vw = lax.axis_index("depth"), lax.axis_index("views")
    x, z = depth // nz, depth % nz
    y, core = vw // 2, vw % 2

    def at_z(q):
        return (x * nz + q, vw)

    def at_x(q):
        return (q * nz + z, vw)

    def at_y(q):
        return (depth, q * 2 + core)

    partner = (depth, y * 2 + 1 - core)
    z_off, x_off, y_off = spread_order(nz), spread_order(nx), spread_order(ny)

    fetch = [
        pltpu.make_async_copy(src, dst, loads.at[n])
        for n, (src, dst) in enumerate(
            [
                (assign_h, assign), (row_index_h, row_index), (row_weight_h, row_weight),
                (col_index_h, col_index), (col_weight_h, col_weight),
                (density_h, density), (target_h, target),
            ]
        )
    ]
    for copy in fetch:
        copy.start()

    barrier = pltpu.get_barrier_semaphore()
    for o in z_off:
        pl.semaphore_signal(barrier, inc=1, device_id=at_z((z + o) % nz), device_id_type=MESH)
    for o in x_off:
        pl.semaphore_signal(barrier, inc=1, device_id=at_x((x + o) % nx), device_id_type=MESH)
    for o in y_off:
        pl.semaphore_signal(barrier, inc=1, device_id=at_y((y + o) % ny), device_id_type=MESH)
    pl.semaphore_signal(barrier, inc=1, device_id=partner, device_id_type=MESH)

    for copy in fetch[:5]:
        copy.wait()
    pad_i[...] = jnp.full(pad_i.shape, -2, jnp.int32)
    pad_w[...] = jnp.zeros(pad_w.shape, F32)
    for v in range(2):
        a = assign[v]
        pad_i[v : v + 1, 0:pixels] = row_index[pl.ds(a, 1), :]
        pad_w[v : v + 1, 0:pixels] = row_weight[pl.ds(a, 1), :]
        pad_i[2 + v : 3 + v, 0:pixels] = col_index[pl.ds(a, 1), :]
        pad_w[2 + v : 3 + v, 0:pixels] = col_weight[pl.ds(a, 1), :]

    def resampler(row, lanes):
        idx, w = pad_i[row : row + 1, 0:lanes], pad_w[row : row + 1, 0:lanes]
        places = lax.broadcasted_iota(jnp.int32, (cells, lanes), 0)
        zero = jnp.zeros((cells, lanes), F32)
        return jnp.where(places == idx, 1.0 - w, zero) + jnp.where(places == idx + 1, w, zero)

    for v in range(2):
        tall[v] = resampler(v, 2 * cells).T
        ct = resampler(2 + v, wide)
        both = jnp.concatenate([ct, pltpu.roll(ct, pixels, 1)], axis=0)
        cols_m[v] = both.astype(BF)
        cols_t[v] = both.T.astype(BF)
    rows = jnp.concatenate(
        [tall[v, pl.ds(p, half, stride=2), :] for p in range(2) for v in range(2)], axis=0
    )
    rows_m[...] = rows.astype(BF)
    tall_rows = 8 * nz
    for k in range(chunks):
        at = k * tall_rows
        both = jnp.concatenate([rows[p * pixels + at : p * pixels + at + tall_rows] for p in range(2)], axis=0)
        rows_t[k] = both.T.astype(BF)

    def views_in(k):
        out = []
        for v in range(2):
            lo, hi = max(k * tall_rows, v * half), min((k + 1) * tall_rows, (v + 1) * half)
            if lo < hi:
                out.append((v, lo - k * tall_rows, hi - lo))
        return out

    def sample(k):
        at = k * tall_rows
        lhs = jnp.concatenate(
            [rows_m[p * pixels + at : p * pixels + at + tall_rows, :] for p in range(2)], axis=0
        )
        for pair in range(slices // 2):
            two = jnp.concatenate([density[2 * pair], density[2 * pair + 1]], axis=1)
            out = jnp.dot(lhs, two, preferred_element_type=F32).astype(BF)
            for s in range(2):
                cut = out[:, s * cells : (s + 1) * cells]
                crossed[2 * pair + s] = jnp.concatenate([cut[:tall_rows], cut[tall_rows:]], axis=1)
        for v, first, n in views_in(k):
            out = jnp.dot(
                crossed[:, first : first + n, :].reshape(slices * n, 2 * cells),
                cols_m[v],
                preferred_element_type=F32,
            )
            work[:, at + first : at + first + n, :] = out.reshape(slices, n, wide)

    def march(tile, carry):
        at = pl.ds(pl.multiple_of(tile * 8, 8), 8)
        through = jnp.ones((8, wide), F32)
        inclusive = jnp.zeros((8, wide), F32)
        for s in range(slices):
            value = work[s, at, :]
            optical = step * value
            att = jnp.exp2(value * (-step * LOG2E))
            gone = 1.0 - att
            inclusive = inclusive + through * (optical * gone)
            work[s, at, :] = through * (gone + optical * att) + inclusive
            through = through * att
        mine[tile, 0] = inclusive * (1.0 / step)
        mine[tile, 1] = through
        return carry

    pending = []

    def send(src, dst, ssem, rsem, device):
        copy = pltpu.make_async_remote_copy(
            src_ref=src, dst_ref=dst, send_sem=ssem, recv_sem=rsem, device_id=device, device_id_type=MESH
        )
        copy.start()
        return copy

    def arrived(dst, rsem):
        pltpu.make_async_remote_copy(
            src_ref=dst, dst_ref=dst, send_sem=rsem, recv_sem=rsem, device_id=partner, device_id_type=MESH
        ).wait_recv()

    fetch[5].wait()
    for k in range(chunks):
        sample(k)
        lax.fori_loop(k * nz, (k + 1) * nz, march, 0)
        if k == 0:
            pl.semaphore_wait(barrier, len(z_off) + len(x_off) + len(y_off) + 1)
        for o in z_off:
            q = (z + o) % nz
            pending.append(send(mine.at[k * nz + q], theirs.at[k, z], s1.at[k, q], r1.at[k, z], at_z(q)))

    fetch[6].wait()
    groups = wide // 128
    for v in range(2):
        for g in range(groups):
            goal[v * half : (v + 1) * half, g * 128 : (g + 1) * 128] = target[
                pl.ds(2 * g + v, half, stride=2 * groups), :
            ]

    def slab_of(k):
        theirs[k, z] = mine[k * nz + z]
        for o in z_off:
            q = (z + o) % nz
            arrived(theirs.at[k, q], r1.at[k, q])
        c = jnp.zeros((8, wide), F32)
        t = jnp.ones((8, wide), F32)
        for q in range(nz):
            local[k, q, 0] = c
            local[k, q, 1] = t
            c = c + t * theirs[k, q, 0]
            t = t * theirs[k, q, 1]
        slab[k, 0] = c
        slab[k, 1] = t
        slabs[k, x, 0] = c
        slabs[k, x, 1] = t
        for o in x_off:
            q = (x + o) % nx
            pending.append(send(slab.at[k], slabs.at[k, x], s2.at[k, q], r2.at[k, x], at_x(q)))

    def lead_of(k):
        for o in x_off:
            q = (x + o) % nx
            arrived(slabs.at[k, q], r2.at[k, q])
        lead_c = jnp.zeros((8, wide), F32)
        lead_t = jnp.ones((8, wide), F32)
        c, t = lead_c, lead_t
        for q in range(nx):
            c = c + t * slabs[k, q, 0]
            t = t * slabs[k, q, 1]
            earlier = q < x
            lead_c = jnp.where(earlier, c, lead_c)
            lead_t = jnp.where(earlier, t, lead_t)
        own = k * nz + z
        for g in range(groups):

            @pl.when(x == g % nx)
            def _():
                totals[g, own] = c[:, g * 128 : (g + 1) * 128]
                for o in z_off:
                    q = (z + o) % nz
                    send(totals.at[g, own], totals.at[g, own], s6.at[k, g, q], r6.at[k, g, z], at_z(q))

        for q in range(nz):
            back[k, q, 0] = lead_t * local[k, q, 1]
            back[k, q, 1] = c - (lead_c + lead_t * local[k, q, 0])
        for o in z_off:
            q = (z + o) % nz
            pending.append(send(back.at[k, q], final.at[own], s3.at[k, q], r3.at[k, z], at_z(q)))
        final[own] = back[k, z]

    def share_of(k):
        for g in range(groups):

            @pl.when(x == g % nx)
            def _():
                for o in z_off:
                    q = (z + o) % nz
                    arrived(totals.at[g, k * nz + q], r6.at[k, g, q])
                for o in x_off:
                    q = (x + o) % nx
                    tiles = totals.at[g, k * nz : (k + 1) * nz]
                    send(tiles, tiles, s7.at[k, g, q], r7.at[k, g], at_x(q))

    def sent_totals(k):
        for g in range(groups):

            @pl.when(x == g % nx)
            def _():
                one = totals.at[g, k * nz + z]
                tiles = totals.at[g, k * nz : (k + 1) * nz]
                for o in z_off:
                    q = (z + o) % nz
                    pltpu.make_async_remote_copy(
                        src_ref=one, dst_ref=one, send_sem=s6.at[k, g, q], recv_sem=r6.at[k, g, z],
                        device_id=at_z(q), device_id_type=MESH,
                    ).wait_send()
                for o in x_off:
                    q = (x + o) % nx
                    pltpu.make_async_remote_copy(
                        src_ref=tiles, dst_ref=tiles, send_sem=s7.at[k, g, q], recv_sem=r7.at[k, g],
                        device_id=at_x(q), device_id_type=MESH,
                    ).wait_send()

    def weigh(k):
        for o in z_off:
            q = (z + o) % nz
            arrived(final.at[k * nz + q], r3.at[k, q])
        for g in range(groups):

            @pl.when(x != g % nx)
            def _():
                arrived(totals.at[g, k * nz : (k + 1) * nz], r7.at[k, g])

        at = slice(k * tall_rows, (k + 1) * tall_rows)
        tiles = slice(k * nz, (k + 1) * nz)
        total = jnp.concatenate([totals[g, tiles].reshape(tall_rows, 128) for g in range(groups)], axis=1)
        residue = levels * (total - goal[at])
        gain[at] = residue * final[tiles, 0].reshape(tall_rows, wide)
        shift[at] = step * residue * final[tiles, 1].reshape(tall_rows, wide)

    def terms(k, first, count):
        at = slice(k * tall_rows, (k + 1) * tall_rows)
        g = [(gain[at] * work[first + s, at] - shift[at]).astype(BF) for s in range(count)]
        spread = [
            (
                n,
                jnp.dot(
                    jnp.concatenate([g[s][a : a + n] for s in range(count)], axis=0),
                    cols_t[v],
                    preferred_element_type=F32,
                ).astype(BF),
            )
            for v, a, n in views_in(k)
        ]
        out = []
        for pair in range(0, count, 2):
            stack = jnp.concatenate(
                [
                    jnp.concatenate(
                        [
                            value[s * n : (s + 1) * n, p * cells : (p + 1) * cells]
                            for p in range(2)
                            for n, value in spread
                        ],
                        axis=0,
                    )
                    for s in (pair, pair + 1)
                ],
                axis=1,
            )
            both = jnp.dot(rows_t[k], stack, preferred_element_type=F32)
            out += [both[:, :cells], both[:, cells:]]
        return out

    def collect(k):
        def body(i, carry):
            for s, value in enumerate(terms(k, 4 * i, 4)):
                part[4 * i + s] = value if k == 0 else part[4 * i + s] + value
            return carry

        lax.fori_loop(0, slices // 4, body, 0)

    last = chunks - 1
    steps = []
    for k in range(chunks):
        steps += [(slab_of, k), (lead_of, k)]
        if k >= 1 and k < last:
            steps.append((share_of, k - 1))
    steps += [(share_of, last - 1)]
    for k in range(last):
        if k == 1 or last == 1:
            steps.append((share_of, last))
        steps += [(weigh, k), (collect, k)]
    steps.append((weigh, last))
    for do, k in steps:
        do(k)

    def merge(o):
        q = (y + o) % ny
        arrived(got.at[q], r4.at[q])
        summed[q] = keep[q] + got[q]
        if o:
            pending.append(send(summed.at[q], pieces.at[y], s5.at[q], r5.at[y], at_y(q)))

    order = y_off[::-1] + [0]
    for n, o in enumerate(order):
        q = (y + o) % ny
        for i in range(0, share, 2):
            first = (2 * q + 1 - core) * share + i
            for s, value in enumerate(terms(last, first, 2)):
                give[q, i + s] = part[first + s] + value
        pending.append(send(give.at[q], got.at[q], s4.at[q], r4.at[q], partner))
        for i in range(0, share, 2):
            first = (2 * q + core) * share + i
            for s, value in enumerate(terms(last, first, 2)):
                keep[q, i + s] = part[first + s] + value
        if n:
            merge(order[n - 1])
    merge(0)

    per = half // 8
    for v in range(2):
        for g in range(groups):
            image[pl.ds(2 * g + v, half, stride=2 * groups), :] = totals[
                g, v * per : (v + 1) * per
            ].reshape(half, 128)

    total = summed[y]
    for o in y_off:
        q = (y + o) % ny
        arrived(pieces.at[q], r5.at[q])
        total = total + pieces[q]
    grad[...] = total
    for copy in pending:
        copy.wait_send()
    for k in range(chunks):
        sent_totals(k)


def on_device(nx, nz, ny, density, row_index, row_weight, col_index, col_weight, assignment, target_image):
    slices, cells = density.shape[0], density.shape[1]
    views, flat = target_image.shape
    pixels = row_index.shape[1]
    wide, tiles = 2 * pixels, flat * views // (8 * 2 * pixels)
    chunks = tiles // nz
    share = slices // (2 * ny)
    lines = flat // 128
    vm = pl.BlockSpec(memory_space=pltpu.VMEM)
    dma = pltpu.SemaphoreType.DMA
    image, grad = pl.pallas_call(
        functools.partial(kernel, (nx, nz, ny, slices * nx * nz)),
        out_shape=(
            jax.ShapeDtypeStruct((views * lines, 128), F32),
            jax.ShapeDtypeStruct((share, cells, cells), F32),
        ),
        in_specs=[pl.BlockSpec(memory_space=pltpu.HBM)] * 7,
        out_specs=(vm, vm),
        scratch_shapes=[
            pltpu.SMEM(assignment.shape, jnp.int32),
            pltpu.VMEM(density.shape, BF),
            pltpu.VMEM(row_index.shape, jnp.int32),
            pltpu.VMEM(row_index.shape, F32),
            pltpu.VMEM(row_index.shape, jnp.int32),
            pltpu.VMEM(row_index.shape, F32),
            pltpu.VMEM((views * lines, 128), F32),
            dma((7,)),
            pltpu.VMEM((8, wide), jnp.int32),
            pltpu.VMEM((8, wide), F32),
            pltpu.VMEM((2, 2 * cells, cells), F32),
            pltpu.VMEM((wide, cells), BF),
            pltpu.VMEM((chunks, cells, 16 * nz), BF),
            pltpu.VMEM((2, 2 * cells, wide), BF),
            pltpu.VMEM((2, wide, 2 * cells), BF),
            pltpu.VMEM((slices, 8 * nz, 2 * cells), BF),
            pltpu.VMEM((slices, pixels, wide), F32),
            pltpu.VMEM((pixels, wide), F32),
            pltpu.VMEM((pixels, wide), F32),
            pltpu.VMEM((pixels, wide), F32),
            pltpu.VMEM((tiles, 2, 8, wide), F32),
            pltpu.VMEM((chunks, nz, 2, 8, wide), F32),
            pltpu.VMEM((chunks, nz, 2, 8, wide), F32),
            pltpu.VMEM((chunks, 2, 8, wide), F32),
            pltpu.VMEM((chunks, nx, 2, 8, wide), F32),
            pltpu.VMEM((chunks, nz, 2, 8, wide), F32),
            pltpu.VMEM((tiles, 2, 8, wide), F32),
            pltpu.VMEM((wide // 128, tiles, 8, 128), F32),
            pltpu.VMEM((slices, cells, cells), F32),
            pltpu.VMEM((ny, share, cells, cells), F32),
            pltpu.VMEM((ny, share, cells, cells), F32),
            pltpu.VMEM((ny, share, cells, cells), F32),
            pltpu.VMEM((ny, share, cells, cells), F32),
            pltpu.VMEM((ny, share, cells, cells), F32),
            dma((chunks, nz)), dma((chunks, nz)),
            dma((chunks, nx)), dma((chunks, nx)),
            dma((chunks, nz)), dma((chunks, nz)),
            dma((ny,)), dma((ny,)),
            dma((ny,)), dma((ny,)),
            dma((chunks, wide // 128, nz)), dma((chunks, wide // 128, nz)),
            dma((chunks, wide // 128, nx)), dma((chunks, wide // 128)),
        ],
        compiler_params=pltpu.CompilerParams(
            collective_id=0, has_side_effects=True, vmem_limit_bytes=67043328
        ),
    )(
        assignment, density, row_index, row_weight, col_index, col_weight,
        target_image.reshape(views, lines, 128).transpose(1, 0, 2).reshape(views * lines, 128),
    )
    return image.reshape(lines, views, 128).transpose(1, 0, 2).reshape(views, flat), grad


def solution(mesh, nz=ZDEV):
    placed = (P("depth", None, None), P(), P(), P(), P(), P("views"), P("views", None))
    nx, ny = mesh.shape["depth"] // nz, mesh.shape["views"] // 2
    return jax.shard_map(
        functools.partial(on_device, nx, nz, ny),
        mesh=mesh,
        in_specs=placed,
        out_specs=(P("views", None), P(("depth", "views"), None, None)),
        check_vma=False,
    )
```

```python
import functools

import jax
import jax.numpy as jnp
from jax import lax
from jax.experimental import pallas as pl
from jax.experimental.pallas import tpu as pltpu
from jax.sharding import PartitionSpec as P

MESH = pl.DeviceIdType.MESH
ZDEV = 8
BF = jnp.bfloat16
F32 = jnp.float32
LOG2E = 1.4426950408889634


def spread_order(n):
    out = []
    for k in range(1, n // 2 + 1):
        for o in (k, n - k):
            if o not in out and 0 < o < n:
                out.append(o)
    return out


def kernel(
    dims, *refs
):
    (
    assign_h, density_h, row_index_h, row_weight_h, col_index_h, col_weight_h, target_h, image, grad,
    assign, density, row_index, row_weight, col_index, col_weight, target, loads,
    pad_i, pad_w, tall, rows_m, rows_t, cols_m, cols_t, crossed, work, goal, gain, shift,
    mine, theirs, local, slab, slabs, back, final, totals, part, ended, got, summed, pieces,
    s1, r1, s2, r2, s3, r3, s4, r4, s5, r5, s6, r6, s7, r7,
    ) = refs
    nx, nz, ny, levels = dims
    step = 1.5 / levels
    slices, cells = density.shape[0], density.shape[1]
    half = row_index.shape[1] // 2
    pixels = 2 * half
    wide = 2 * pixels
    chunks = 2 * half // 8 // nz
    share = slices // (2 * ny)
    depth, vw = lax.axis_index("depth"), lax.axis_index("views")
    x, z = depth // nz, depth % nz
    y, core = vw // 2, vw % 2

    def at_z(q):
        return (x * nz + q, vw)

    def at_x(q):
        return (q * nz + z, vw)

    def at_y(q):
        return (depth, q * 2 + core)

    partner = (depth, y * 2 + 1 - core)
    z_off, x_off, y_off = spread_order(nz), spread_order(nx), spread_order(ny)

    fetch = [
        pltpu.make_async_copy(src, dst, loads.at[n])
        for n, (src, dst) in enumerate(
            [
                (assign_h, assign), (row_index_h, row_index), (row_weight_h, row_weight),
                (col_index_h, col_index), (col_weight_h, col_weight),
                (density_h, density), (target_h, target),
            ]
        )
    ]
    for copy in fetch:
        copy.start()

    barrier = pltpu.get_barrier_semaphore()
    for o in z_off:
        pl.semaphore_signal(barrier, inc=1, device_id=at_z((z + o) % nz), device_id_type=MESH)
    for o in x_off:
        pl.semaphore_signal(barrier, inc=1, device_id=at_x((x + o) % nx), device_id_type=MESH)
    for o in y_off:
        pl.semaphore_signal(barrier, inc=1, device_id=at_y((y + o) % ny), device_id_type=MESH)
    pl.semaphore_signal(barrier, inc=1, device_id=partner, device_id_type=MESH)

    for copy in fetch[:5]:
        copy.wait()
    pad_i[...] = jnp.full(pad_i.shape, -2, jnp.int32)
    pad_w[...] = jnp.zeros(pad_w.shape, F32)
    for v in range(2):
        a = assign[v]
        pad_i[v : v + 1, 0:pixels] = row_index[pl.ds(a, 1), :]
        pad_w[v : v + 1, 0:pixels] = row_weight[pl.ds(a, 1), :]
        pad_i[2 + v : 3 + v, 0:pixels] = col_index[pl.ds(a, 1), :]
        pad_w[2 + v : 3 + v, 0:pixels] = col_weight[pl.ds(a, 1), :]

    def resampler(row, lanes):
        idx, w = pad_i[row : row + 1, 0:lanes], pad_w[row : row + 1, 0:lanes]
        places = lax.broadcasted_iota(jnp.int32, (cells, lanes), 0)
        zero = jnp.zeros((cells, lanes), F32)
        return jnp.where(places == idx, 1.0 - w, zero) + jnp.where(places == idx + 1, w, zero)

    tall_rows = 8 * nz

    def resamplers(v):
        tall[v] = resampler(v, 2 * cells).T
        for p in range(2):
            rows_m[p * pixels + v * half : p * pixels + (v + 1) * half, :] = tall[
                v, pl.ds(p, half, stride=2), :
            ].astype(BF)
        ct = resampler(2 + v, wide)
        cols_m[v] = jnp.concatenate([ct, pltpu.roll(ct, pixels, 1)], axis=0).astype(BF)

    def transposed():
        for v in range(2):
            cols_t[v] = cols_m[v].T
        for k in range(chunks):
            at = k * tall_rows
            rows_t[k] = jnp.concatenate(
                [rows_m[p * pixels + at : p * pixels + at + tall_rows, :] for p in range(2)], axis=0
            ).T

    def views_in(k):
        out = []
        for v in range(2):
            lo, hi = max(k * tall_rows, v * half), min((k + 1) * tall_rows, (v + 1) * half)
            if lo < hi:
                out.append((v, lo - k * tall_rows, hi - lo))
        return out

    def sample(k):
        at = k * tall_rows
        lhs = jnp.concatenate(
            [rows_m[p * pixels + at : p * pixels + at + tall_rows, :] for p in range(2)], axis=0
        )
        for pair in range(slices // 2):
            two = jnp.concatenate([density[2 * pair], density[2 * pair + 1]], axis=1)
            out = jnp.dot(lhs, two, preferred_element_type=F32).astype(BF)
            for s in range(2):
                cut = out[:, s * cells : (s + 1) * cells]
                crossed[2 * pair + s] = jnp.concatenate([cut[:tall_rows], cut[tall_rows:]], axis=1)
        for v, first, n in views_in(k):
            out = jnp.dot(
                crossed[:, first : first + n, :].reshape(slices * n, 2 * cells),
                cols_m[v],
                preferred_element_type=F32,
            )
            work[:, at + first : at + first + n, :] = out.reshape(slices, n, wide)

    def march(tile):
        at = pl.ds(pl.multiple_of(tile * 8, 8), 8)
        through = jnp.ones((8, wide), F32)
        inclusive = jnp.zeros((8, wide), F32)
        for s in range(slices):
            value = work[s, at, :]
            optical = step * value
            att = jnp.exp2(value * (-step * LOG2E))
            gone = 1.0 - att
            inclusive = inclusive + through * (optical * gone)
            work[s, at, :] = through * (gone + optical * att) + inclusive
            through = through * att
        mine[tile, 0] = inclusive * (1.0 / step)
        mine[tile, 1] = through

    pending = []

    def send(src, dst, ssem, rsem, device):
        copy = pltpu.make_async_remote_copy(
            src_ref=src, dst_ref=dst, send_sem=ssem, recv_sem=rsem, device_id=device, device_id_type=MESH
        )
        copy.start()
        return copy

    def arrived(dst, rsem):
        pltpu.make_async_remote_copy(
            src_ref=dst, dst_ref=dst, send_sem=rsem, recv_sem=rsem, device_id=partner, device_id_type=MESH
        ).wait_recv()

    fetch[5].wait()
    built = 0
    for k in range(chunks):
        for v, _, _ in views_in(k):
            if v >= built:
                resamplers(v)
                built = v + 1
        sample(k)
        for o in z_off:
            q = (z + o) % nz
            march(k * nz + q)
            if k == 0 and o == z_off[0]:
                pl.semaphore_wait(barrier, len(z_off) + len(x_off) + len(y_off) + 1)
            pending.append(send(mine.at[k * nz + q], theirs.at[k, z], s1.at[k, q], r1.at[k, z], at_z(q)))
        march(k * nz + z)
    transposed()

    fetch[6].wait()
    groups = wide // 128
    for v in range(2):
        for g in range(groups):
            goal[v * half : (v + 1) * half, g * 128 : (g + 1) * 128] = target[
                pl.ds(2 * g + v, half, stride=2 * groups), :
            ]

    def slab_of(k):
        theirs[k, z] = mine[k * nz + z]
        for o in z_off:
            q = (z + o) % nz
            arrived(theirs.at[k, q], r1.at[k, q])
        c = jnp.zeros((8, wide), F32)
        t = jnp.ones((8, wide), F32)
        for q in range(nz):
            local[k, q, 0] = c
            local[k, q, 1] = t
            c = c + t * theirs[k, q, 0]
            t = t * theirs[k, q, 1]
        slab[k, 0] = c
        slab[k, 1] = t
        slabs[k, x, 0] = c
        slabs[k, x, 1] = t
        for o in x_off:
            q = (x + o) % nx
            pending.append(send(slab.at[k], slabs.at[k, x], s2.at[k, q], r2.at[k, x], at_x(q)))

    def lead_of(k):
        for o in x_off:
            q = (x + o) % nx
            arrived(slabs.at[k, q], r2.at[k, q])
        lead_c = jnp.zeros((8, wide), F32)
        lead_t = jnp.ones((8, wide), F32)
        c, t = lead_c, lead_t
        for q in range(nx):
            c = c + t * slabs[k, q, 0]
            t = t * slabs[k, q, 1]
            earlier = q < x
            lead_c = jnp.where(earlier, c, lead_c)
            lead_t = jnp.where(earlier, t, lead_t)
        own = k * nz + z
        for g in range(groups):

            @pl.when(x == g % nx)
            def _():
                totals[g, own] = c[:, g * 128 : (g + 1) * 128]
                for o in z_off:
                    q = (z + o) % nz
                    send(totals.at[g, own], totals.at[g, own], s6.at[k, g, q], r6.at[k, g, z], at_z(q))

        for q in range(nz):
            back[k, q, 0] = lead_t * local[k, q, 1]
            back[k, q, 1] = c - (lead_c + lead_t * local[k, q, 0])
        for o in z_off:
            q = (z + o) % nz
            pending.append(send(back.at[k, q], final.at[own], s3.at[k, q], r3.at[k, z], at_z(q)))
        final[own] = back[k, z]

    def share_of(k):
        for g in range(groups):

            @pl.when(x == g % nx)
            def _():
                for o in z_off:
                    q = (z + o) % nz
                    arrived(totals.at[g, k * nz + q], r6.at[k, g, q])
                for o in x_off:
                    q = (x + o) % nx
                    tiles = totals.at[g, k * nz : (k + 1) * nz]
                    send(tiles, tiles, s7.at[k, g, q], r7.at[k, g], at_x(q))

    def sent_totals(k):
        for g in range(groups):

            @pl.when(x == g % nx)
            def _():
                one = totals.at[g, k * nz + z]
                tiles = totals.at[g, k * nz : (k + 1) * nz]
                for o in z_off:
                    q = (z + o) % nz
                    pltpu.make_async_remote_copy(
                        src_ref=one, dst_ref=one, send_sem=s6.at[k, g, q], recv_sem=r6.at[k, g, z],
                        device_id=at_z(q), device_id_type=MESH,
                    ).wait_send()
                for o in x_off:
                    q = (x + o) % nx
                    pltpu.make_async_remote_copy(
                        src_ref=tiles, dst_ref=tiles, send_sem=s7.at[k, g, q], recv_sem=r7.at[k, g],
                        device_id=at_x(q), device_id_type=MESH,
                    ).wait_send()

    def weigh(k):
        for o in z_off:
            q = (z + o) % nz
            arrived(final.at[k * nz + q], r3.at[k, q])
        for g in range(groups):

            @pl.when(x != g % nx)
            def _():
                arrived(totals.at[g, k * nz : (k + 1) * nz], r7.at[k, g])

        at = slice(k * tall_rows, (k + 1) * tall_rows)
        tiles = slice(k * nz, (k + 1) * nz)
        total = jnp.concatenate([totals[g, tiles].reshape(tall_rows, 128) for g in range(groups)], axis=1)
        residue = levels * (total - goal[at])
        gain[at] = residue * final[tiles, 0].reshape(tall_rows, wide)
        shift[at] = step * residue * final[tiles, 1].reshape(tall_rows, wide)

    def terms(k, first, count):
        at = slice(k * tall_rows, (k + 1) * tall_rows)
        g = [(gain[at] * work[first + s, at] - shift[at]).astype(BF) for s in range(count)]
        spread = [
            (
                n,
                jnp.dot(
                    jnp.concatenate([g[s][a : a + n] for s in range(count)], axis=0),
                    cols_t[v],
                    preferred_element_type=F32,
                ).astype(BF),
            )
            for v, a, n in views_in(k)
        ]
        out = []
        for pair in range(0, count, 2):
            stack = jnp.concatenate(
                [
                    jnp.concatenate(
                        [
                            value[s * n : (s + 1) * n, p * cells : (p + 1) * cells]
                            for p in range(2)
                            for n, value in spread
                        ],
                        axis=0,
                    )
                    for s in (pair, pair + 1)
                ],
                axis=1,
            )
            both = jnp.dot(rows_t[k], stack, preferred_element_type=F32)
            out += [both[:, :cells], both[:, cells:]]
        return out

    def collect(k):
        def body(i, carry):
            for s, value in enumerate(terms(k, 4 * i, 4)):
                part[4 * i + s] = value if k == 0 else part[4 * i + s] + value
            return carry

        lax.fori_loop(0, slices // 4, body, 0)

    last = chunks - 1
    steps = []
    for k in range(chunks):
        steps += [(slab_of, k), (lead_of, k)]
        if k >= 1 and k < last:
            steps.append((share_of, k - 1))
    steps += [(share_of, last - 1)]
    for k in range(last):
        if k == 1 or last == 1:
            steps.append((share_of, last))
        steps += [(weigh, k), (collect, k)]
    steps.append((weigh, last))
    for do, k in steps:
        do(k)

    def merge(o):
        q = (y + o) % ny
        arrived(got.at[q], r4.at[q])
        summed[q] = ended[q, pl.ds(core * share, share)] + got[q]
        if o:
            pending.append(send(summed.at[q], pieces.at[y], s5.at[q], r5.at[y], at_y(q)))

    order = y_off[::-1] + [0]
    for n, o in enumerate(order):
        q = (y + o) % ny
        first = 2 * q * share
        for s, value in enumerate(terms(last, first, 2 * share)):
            ended[q, s] = part[first + s] + value
        pending.append(
            send(ended.at[q, pl.ds((1 - core) * share, share)], got.at[q], s4.at[q], r4.at[q], partner)
        )
        if n:
            merge(order[n - 1])
    merge(0)

    per = half // 8
    for v in range(2):
        for g in range(groups):
            image[pl.ds(2 * g + v, half, stride=2 * groups), :] = totals[
                g, v * per : (v + 1) * per
            ].reshape(half, 128)

    total = summed[y]
    for o in y_off:
        q = (y + o) % ny
        arrived(pieces.at[q], r5.at[q])
        total = total + pieces[q]
    grad[...] = total
    for copy in pending:
        copy.wait_send()
    for k in range(chunks):
        sent_totals(k)


def on_device(nx, nz, ny, density, row_index, row_weight, col_index, col_weight, assignment, target_image):
    slices, cells = density.shape[0], density.shape[1]
    views, flat = target_image.shape
    pixels = row_index.shape[1]
    wide, tiles = 2 * pixels, flat * views // (8 * 2 * pixels)
    chunks = tiles // nz
    share = slices // (2 * ny)
    lines = flat // 128
    vm = pl.BlockSpec(memory_space=pltpu.VMEM)
    dma = pltpu.SemaphoreType.DMA
    image, grad = pl.pallas_call(
        functools.partial(kernel, (nx, nz, ny, slices * nx * nz)),
        out_shape=(
            jax.ShapeDtypeStruct((views * lines, 128), F32),
            jax.ShapeDtypeStruct((share, cells, cells), F32),
        ),
        in_specs=[pl.BlockSpec(memory_space=pltpu.HBM)] * 7,
        out_specs=(vm, vm),
        scratch_shapes=[
            pltpu.SMEM(assignment.shape, jnp.int32),
            pltpu.VMEM(density.shape, BF),
            pltpu.VMEM(row_index.shape, jnp.int32),
            pltpu.VMEM(row_index.shape, F32),
            pltpu.VMEM(row_index.shape, jnp.int32),
            pltpu.VMEM(row_index.shape, F32),
            pltpu.VMEM((views * lines, 128), F32),
            dma((7,)),
            pltpu.VMEM((8, wide), jnp.int32),
            pltpu.VMEM((8, wide), F32),
            pltpu.VMEM((2, 2 * cells, cells), F32),
            pltpu.VMEM((wide, cells), BF),
            pltpu.VMEM((chunks, cells, 16 * nz), BF),
            pltpu.VMEM((2, 2 * cells, wide), BF),
            pltpu.VMEM((2, wide, 2 * cells), BF),
            pltpu.VMEM((slices, 8 * nz, 2 * cells), BF),
            pltpu.VMEM((slices, pixels, wide), F32),
            pltpu.VMEM((pixels, wide), F32),
            pltpu.VMEM((pixels, wide), F32),
            pltpu.VMEM((pixels, wide), F32),
            pltpu.VMEM((tiles, 2, 8, wide), F32),
            pltpu.VMEM((chunks, nz, 2, 8, wide), F32),
            pltpu.VMEM((chunks, nz, 2, 8, wide), F32),
            pltpu.VMEM((chunks, 2, 8, wide), F32),
            pltpu.VMEM((chunks, nx, 2, 8, wide), F32),
            pltpu.VMEM((chunks, nz, 2, 8, wide), F32),
            pltpu.VMEM((tiles, 2, 8, wide), F32),
            pltpu.VMEM((wide // 128, tiles, 8, 128), F32),
            pltpu.VMEM((slices, cells, cells), F32),
            pltpu.VMEM((ny, 2 * share, cells, cells), F32),
            pltpu.VMEM((ny, share, cells, cells), F32),
            pltpu.VMEM((ny, share, cells, cells), F32),
            pltpu.VMEM((ny, share, cells, cells), F32),
            dma((chunks, nz)), dma((chunks, nz)),
            dma((chunks, nx)), dma((chunks, nx)),
            dma((chunks, nz)), dma((chunks, nz)),
            dma((ny,)), dma((ny,)),
            dma((ny,)), dma((ny,)),
            dma((chunks, wide // 128, nz)), dma((chunks, wide // 128, nz)),
            dma((chunks, wide // 128, nx)), dma((chunks, wide // 128)),
        ],
        compiler_params=pltpu.CompilerParams(
            collective_id=0, has_side_effects=True, vmem_limit_bytes=50331648
        ),
    )(*[pltpu.with_memory_space_constraint(a, pltpu.HBM) for a in (
        assignment, density, row_index, row_weight, col_index, col_weight,
        target_image.reshape(views, lines, 128).transpose(1, 0, 2).reshape(views * lines, 128),
    )])
    return image.reshape(lines, views, 128).transpose(1, 0, 2).reshape(views, flat), grad


def solution(mesh, nz=ZDEV):
    placed = (P("depth", None, None), P(), P(), P(), P(), P("views"), P("views", None))
    nx, ny = mesh.shape["depth"] // nz, mesh.shape["views"] // 2
    return jax.shard_map(
        functools.partial(on_device, nx, nz, ny),
        mesh=mesh,
        in_specs=placed,
        out_specs=(P("views", None), P(("depth", "views"), None, None)),
        check_vma=False,
    )
```

```python
import functools

import jax
import jax.numpy as jnp
from jax import lax
from jax.experimental import pallas as pl
from jax.experimental.pallas import tpu as pltpu
from jax.sharding import PartitionSpec as P

MESH = pl.DeviceIdType.MESH
ZDEV = 8
BF = jnp.bfloat16
F32 = jnp.float32
LOG2E = 1.4426950408889634


def spread_order(n):
    out = []
    for k in range(1, n // 2 + 1):
        for o in (k, n - k):
            if o not in out and 0 < o < n:
                out.append(o)
    return out


def kernel(
    dims, *refs
):
    (
    assign_h, density_h, row_index_h, row_weight_h, col_index_h, col_weight_h, target_h, image, grad,
    assign, density, row_index, row_weight, col_index, col_weight, target, loads,
    pad_i, pad_w, tall, rows_m, rows_t, cols_m, cols_t, crossed, work, goal, gain, shift,
    mine, theirs, local, slab, slabs, back, final, totals, part, ended, got, summed, pieces, relay, passed,
    mass, masses, slab_mass, slab_masses, before, ahead,
    s1, r1, s2, r2, s3, r3, s4, r4, s5, r5, s6, r6, s7, r7, s8, r8, s9, r9, s10, r10, s11, r11,
    ) = refs
    nx, nz, ny, levels = dims
    step = 1.5 / levels
    slices, cells = density.shape[0], density.shape[1]
    half = row_index.shape[1] // 2
    pixels = 2 * half
    wide = 2 * pixels
    chunks = 2 * half // 8 // nz
    share = slices // (2 * ny)
    groups = wide // 128
    last = chunks - 1
    units = [(k, slice(0, groups)) for k in range(last)] + [(last, slice(g, g + 1)) for g in range(groups)]
    depth, vw = lax.axis_index("depth"), lax.axis_index("views")
    x, z = depth // nz, depth % nz
    y, core = vw // 2, vw % 2

    def at_z(q):
        return (x * nz + q, vw)

    def at_x(q):
        return (q * nz + z, vw)

    def at_y(q):
        return (depth, q * 2 + core)

    partner = (depth, y * 2 + 1 - core)
    beside = spread_order(2 * ny)
    rows_held = cells // (2 * ny)
    z_off, x_off, y_off = spread_order(nz), spread_order(nx), spread_order(ny)

    fetch = [
        pltpu.make_async_copy(src, dst, loads.at[n])
        for n, (src, dst) in enumerate(
            [
                (assign_h, assign), (row_index_h, row_index), (row_weight_h, row_weight),
                (col_index_h, col_index), (col_weight_h, col_weight),
                (density_h, density), (target_h, target),
            ]
        )
    ]
    for copy in fetch:
        copy.start()

    barrier = pltpu.get_barrier_semaphore()
    for o in z_off:
        pl.semaphore_signal(barrier, inc=1, device_id=at_z((z + o) % nz), device_id_type=MESH)
    for o in x_off:
        pl.semaphore_signal(barrier, inc=1, device_id=at_x((x + o) % nx), device_id_type=MESH)
    for o in beside:
        pl.semaphore_signal(barrier, inc=1, device_id=(depth, (vw + o) % (2 * ny)), device_id_type=MESH)

    for copy in fetch[:5]:
        copy.wait()
    pad_i[...] = jnp.full(pad_i.shape, -2, jnp.int32)
    pad_w[...] = jnp.zeros(pad_w.shape, F32)
    for v in range(2):
        a = assign[v]
        pad_i[v : v + 1, 0:pixels] = row_index[pl.ds(a, 1), :]
        pad_w[v : v + 1, 0:pixels] = row_weight[pl.ds(a, 1), :]
        pad_i[2 + v : 3 + v, 0:pixels] = col_index[pl.ds(a, 1), :]
        pad_w[2 + v : 3 + v, 0:pixels] = col_weight[pl.ds(a, 1), :]

    def resampler(row, lanes):
        idx, w = pad_i[row : row + 1, 0:lanes], pad_w[row : row + 1, 0:lanes]
        places = lax.broadcasted_iota(jnp.int32, (cells, lanes), 0)
        zero = jnp.zeros((cells, lanes), F32)
        return jnp.where(places == idx, 1.0 - w, zero) + jnp.where(places == idx + 1, w, zero)

    tall_rows = 8 * nz

    def resamplers(v):
        tall[v] = resampler(v, 2 * cells).T
        for p in range(2):
            rows_m[p * pixels + v * half : p * pixels + (v + 1) * half, :] = tall[
                v, pl.ds(p, half, stride=2), :
            ].astype(BF)
        ct = resampler(2 + v, wide)
        cols_m[v] = jnp.concatenate([ct, pltpu.roll(ct, pixels, 1)], axis=0).astype(BF)

    def transposed():
        for v in range(2):
            cols_t[v] = cols_m[v].T
        for k in range(chunks):
            at = k * tall_rows
            rows_t[k] = jnp.concatenate(
                [rows_m[p * pixels + at : p * pixels + at + tall_rows, :] for p in range(2)], axis=0
            ).T

    def views_in(k):
        out = []
        for v in range(2):
            lo, hi = max(k * tall_rows, v * half), min((k + 1) * tall_rows, (v + 1) * half)
            if lo < hi:
                out.append((v, lo - k * tall_rows, hi - lo))
        return out

    def sample(k):
        at = k * tall_rows
        lhs = jnp.concatenate(
            [rows_m[p * pixels + at : p * pixels + at + tall_rows, :] for p in range(2)], axis=0
        )
        for pair in range(slices // 2):
            two = jnp.concatenate([density[2 * pair], density[2 * pair + 1]], axis=1)
            out = jnp.dot(lhs, two, preferred_element_type=F32).astype(BF)
            for s in range(2):
                cut = out[:, s * cells : (s + 1) * cells]
                crossed[2 * pair + s] = jnp.concatenate([cut[:tall_rows], cut[tall_rows:]], axis=1)
        for v, first, n in views_in(k):
            out = jnp.dot(
                crossed[:, first : first + n, :].reshape(slices * n, 2 * cells),
                cols_m[v],
                preferred_element_type=F32,
            )
            work[:, at + first : at + first + n, :] = out.reshape(slices, n, wide)

    def march(tile):
        at = pl.ds(pl.multiple_of(tile * 8, 8), 8)
        through = jnp.ones((8, wide), F32)
        inclusive = jnp.zeros((8, wide), F32)
        for s in range(slices):
            value = work[s, at, :]
            optical = step * value
            att = jnp.exp2(value * (-step * LOG2E))
            gone = 1.0 - att
            inclusive = inclusive + through * (optical * gone)
            work[s, at, :] = through * (gone + optical * att) + inclusive
            through = through * att
        for g in range(groups):
            lanes = slice(g * 128, (g + 1) * 128)
            mine[tile, g, 0] = inclusive[:, lanes] * (1.0 / step)
            mine[tile, g, 1] = through[:, lanes]

    pending = []

    def send(src, dst, ssem, rsem, device):
        copy = pltpu.make_async_remote_copy(
            src_ref=src, dst_ref=dst, send_sem=ssem, recv_sem=rsem, device_id=device, device_id_type=MESH
        )
        copy.start()
        return copy

    def arrived(dst, rsem):
        pltpu.make_async_remote_copy(
            src_ref=dst, dst_ref=dst, send_sem=rsem, recv_sem=rsem, device_id=partner, device_id_type=MESH
        ).wait_recv()

    def mass_sent():
        held = density[:, pl.ds(pl.multiple_of(vw * rows_held, rows_held), rows_held), :]
        one = jnp.sum(held.astype(F32), axis=0)
        mass[...] = one
        masses[z] = one
        for o in z_off:
            q = (z + o) % nz
            pending.append(send(mass, masses.at[z], s8.at[q], r8.at[z], at_z(q)))

    def mass_along_z():
        for o in z_off:
            q = (z + o) % nz
            arrived(masses.at[q], r8.at[q])
        lead = jnp.zeros((rows_held, cells), F32)
        total = lead
        for q in range(nz):
            lead = jnp.where(q == z, total, lead)
            total = total + masses[q]
        slab_mass[...] = total
        before[vw] = lead
        for o in x_off:
            q = (x + o) % nx
            pending.append(send(slab_mass, slab_masses.at[x], s9.at[q], r9.at[x], at_x(q)))

    def mass_along_x():
        slab_masses[x] = jnp.zeros((rows_held, cells), F32)
        for o in x_off:
            q = (x + o) % nx
            arrived(slab_masses.at[q], r9.at[q])
        lead = before[vw]
        for q in range(nx):
            lead = lead + jnp.where(q < x, slab_masses[q], 0.0)
        before[vw] = lead
        for o in beside:
            q = (vw + o) % (2 * ny)
            pending.append(send(before.at[vw], before.at[vw], s10.at[q], r10.at[vw], (depth, q)))

    def split(value):
        high = value.astype(BF)
        return high, (value - high.astype(F32)).astype(BF)

    def see_ahead():
        for o in beside:
            q = (vw + o) % (2 * ny)
            arrived(before.at[q], r10.at[q])
        two = jnp.concatenate(split(before[...].reshape(cells, cells)), axis=1)
        out = jnp.dot(rows_m[...], two, preferred_element_type=F32)
        out = out[:, :cells] + out[:, cells:]
        parts = split(jnp.concatenate([out[:pixels], out[pixels:]], axis=1))
        for v in range(2):
            at = slice(v * half, (v + 1) * half)
            passed = sum(jnp.dot(part[at], cols_m[v], preferred_element_type=F32) for part in parts)
            ahead[at] = jnp.exp2(passed * (-step * LOG2E))

    def send_share(u, q):
        k, gs = units[u]
        pending.append(
            send(mine.at[k * nz + q, gs], theirs.at[k, z, gs], s1.at[u, q], r1.at[u, z], at_z(q))
        )

    built = 0
    for k in range(chunks):
        for v, _, _ in views_in(k):
            if v >= built:
                resamplers(v)
                built = v + 1
        if k == 0:
            fetch[5].wait()
        sample(k)
        for q in range(nz):
            march(k * nz + q)
        if k == 0:
            pl.semaphore_wait(barrier, len(z_off) + len(x_off) + len(beside))
        for u in [k] if k < last else range(last, len(units)):
            for o in z_off:
                send_share(u, (z + o) % nz)
        if k == 0:
            mass_sent()
    transposed()

    fetch[6].wait()
    for v in range(2):
        for g in range(groups):
            goal[v * half : (v + 1) * half, g * 128 : (g + 1) * 128] = target[
                pl.ds(2 * g + v, half, stride=2 * groups), :
            ]

    def slab_of(u):
        k, gs = units[u]
        theirs[k, z, gs] = mine[k * nz + z, gs]
        for o in z_off:
            q = (z + o) % nz
            arrived(theirs.at[k, q, gs], r1.at[u, q])
        c = jnp.zeros((gs.stop - gs.start, 8, 128), F32)
        t = jnp.ones((gs.stop - gs.start, 8, 128), F32)
        for q in range(nz):
            local[k, q, gs] = c
            c = c + t * theirs[k, q, gs, 0]
            t = t * theirs[k, q, gs, 1]
        slab[k, gs, 0] = c
        slab[k, gs, 1] = t
        slabs[k, x, gs, 0] = c
        slabs[k, x, gs, 1] = t
        for o in x_off:
            q = (x + o) % nx
            pending.append(send(slab.at[k, gs], slabs.at[k, x, gs], s2.at[u, q], r2.at[u, x], at_x(q)))

    def lead_of(u):
        k, gs = units[u]
        for o in x_off:
            q = (x + o) % nx
            arrived(slabs.at[k, q, gs], r2.at[u, q])
        lead_c = jnp.zeros((gs.stop - gs.start, 8, 128), F32)
        lead_t = jnp.ones((gs.stop - gs.start, 8, 128), F32)
        c, t = lead_c, lead_t
        for q in range(nx):
            c = c + t * slabs[k, q, gs, 0]
            t = t * slabs[k, q, gs, 1]
            earlier = q < x
            lead_c = jnp.where(earlier, c, lead_c)
            lead_t = jnp.where(earlier, t, lead_t)
        own = k * nz + z
        if k == last:
            g = gs.start
            totals[g, own] = c[0]
            for o in z_off:
                q = (z + o) % nz
                pending.append(
                    send(totals.at[g, own], totals.at[g, own], s6.at[k, g, q], r6.at[k, g, z], at_z(q))
                )
        else:
            for g in range(groups):

                @pl.when(x == g % nx)
                def _():
                    totals[g, own] = c[g]
                    for o in z_off:
                        q = (z + o) % nz
                        send(totals.at[g, own], totals.at[g, own], s6.at[k, g, q], r6.at[k, g, z], at_z(q))

        for q in range(nz):
            back[k, q, gs] = c - (lead_c + lead_t * local[k, q, gs])
        for o in z_off:
            q = (z + o) % nz
            pending.append(send(back.at[k, q, gs], final.at[own, gs], s3.at[u, q], r3.at[u, z], at_z(q)))
        final[own, gs] = back[k, z, gs]

    def share_of(k):
        for g in range(groups):

            @pl.when(x == g % nx)
            def _():
                for o in z_off:
                    q = (z + o) % nz
                    arrived(totals.at[g, k * nz + q], r6.at[k, g, q])
                for o in x_off:
                    q = (x + o) % nx
                    tiles = totals.at[g, k * nz : (k + 1) * nz]
                    send(tiles, tiles, s7.at[k, g, q], r7.at[k, g], at_x(q))

    def sent_totals(k):
        for g in range(groups):

            @pl.when(x == g % nx)
            def _():
                one = totals.at[g, k * nz + z]
                tiles = totals.at[g, k * nz : (k + 1) * nz]
                for o in z_off:
                    q = (z + o) % nz
                    pltpu.make_async_remote_copy(
                        src_ref=one, dst_ref=one, send_sem=s6.at[k, g, q], recv_sem=r6.at[k, g, z],
                        device_id=at_z(q), device_id_type=MESH,
                    ).wait_send()
                for o in x_off:
                    q = (x + o) % nx
                    pltpu.make_async_remote_copy(
                        src_ref=tiles, dst_ref=tiles, send_sem=s7.at[k, g, q], recv_sem=r7.at[k, g],
                        device_id=at_x(q), device_id_type=MESH,
                    ).wait_send()

    def weigh(k):
        for u, (j, gs) in enumerate(units):
            if j == k:
                for o in z_off:
                    q = (z + o) % nz
                    arrived(final.at[k * nz + q, gs], r3.at[u, q])
        for g in range(groups):
            if k == last:
                for o in z_off:
                    q = (z + o) % nz
                    arrived(totals.at[g, k * nz + q], r6.at[k, g, q])
            else:

                @pl.when(x != g % nx)
                def _():
                    arrived(totals.at[g, k * nz : (k + 1) * nz], r7.at[k, g])

        at = slice(k * tall_rows, (k + 1) * tall_rows)
        tiles = slice(k * nz, (k + 1) * nz)
        total = jnp.concatenate([totals[g, tiles].reshape(tall_rows, 128) for g in range(groups)], axis=1)
        residue = levels * (total - goal[at])
        gain[at] = residue * ahead[at]
        behind = jnp.concatenate([final[tiles, g].reshape(tall_rows, 128) for g in range(groups)], axis=1)
        shift[at] = step * residue * behind

    def terms(k, first, count):
        at = slice(k * tall_rows, (k + 1) * tall_rows)
        g = [(gain[at] * work[first + s, at] - shift[at]).astype(BF) for s in range(count)]
        spread = [
            (
                n,
                jnp.dot(
                    jnp.concatenate([g[s][a : a + n] for s in range(count)], axis=0),
                    cols_t[v],
                    preferred_element_type=F32,
                ).astype(BF),
            )
            for v, a, n in views_in(k)
        ]
        out = []
        for pair in range(0, count, 2):
            stack = jnp.concatenate(
                [
                    jnp.concatenate(
                        [
                            value[s * n : (s + 1) * n, p * cells : (p + 1) * cells]
                            for p in range(2)
                            for n, value in spread
                        ],
                        axis=0,
                    )
                    for s in (pair, pair + 1)
                ],
                axis=1,
            )
            both = jnp.dot(rows_t[k], stack, preferred_element_type=F32)
            out += [both[:, :cells], both[:, cells:]]
        return out

    def collect(k):
        def body(i, carry):
            for s, value in enumerate(terms(k, 4 * i, 4)):
                part[4 * i + s] = value if k == 0 else part[4 * i + s] + value
            return carry

        lax.fori_loop(0, slices // 4, body, 0)

    slab_of(0)
    mass_along_z()
    lead_of(0)
    mass_along_x()
    for k in range(1, last):
        slab_of(k)
        if k == last - 1:
            slab_of(last)
        lead_of(k)
        share_of(k - 1)
    see_ahead()
    for u in range(last + 1, len(units)):
        slab_of(u)
    for u in range(last, len(units)):
        lead_of(u)
    share_of(last - 1)
    for k in range(last):
        weigh(k)
        collect(k)
    weigh(last)

    up, down = (y + 1) % ny, (y + ny - 1) % ny
    halves = slice(0, share // 2), slice(share // 2, share)

    def give_half(n, src, q):
        pending.append(send(src, pieces.at[y, halves[n]], s5.at[q, n], r5.at[y, n], at_y(q)))

    def merge(o):
        q = (y + o) % ny
        arrived(got.at[q], r4.at[q])
        summed[q] = ended[q, pl.ds(core * share, share)] + got[q]
        if o == 2:
            for n, near in enumerate((up, down)):
                pending.append(send(summed.at[q, halves[n]], relay.at[n], s11.at[n], r11.at[n], at_y(near)))
        elif o == 1:
            give_half(1, summed.at[q, halves[1]], q)
        elif o == 3:
            give_half(0, summed.at[q, halves[0]], q)

    def pass_on():
        for n, near in enumerate((up, down)):
            arrived(relay.at[n], r11.at[n])
            passed[n] = summed[near, halves[n]] + relay[n]
            give_half(n, passed.at[n], near)

    order = y_off[::-1] + [0]
    for n, o in enumerate(order):
        q = (y + o) % ny
        first = 2 * q * share
        for s, value in enumerate(terms(last, first, 2 * share)):
            ended[q, s] = part[first + s] + value
        pending.append(
            send(ended.at[q, pl.ds((1 - core) * share, share)], got.at[q], s4.at[q], r4.at[q], partner)
        )
        if n:
            merge(order[n - 1])
    merge(0)
    pass_on()

    per = half // 8
    for v in range(2):
        for g in range(groups):
            image[pl.ds(2 * g + v, half, stride=2 * groups), :] = totals[
                g, v * per : (v + 1) * per
            ].reshape(half, 128)

    total = summed[y]
    for q in (down, up):
        for n in range(2):
            arrived(pieces.at[q, halves[n]], r5.at[q, n])
        total = total + pieces[q]
    grad[...] = total
    for copy in pending:
        copy.wait_send()
    for k in range(last):
        sent_totals(k)


def on_device(nx, nz, ny, density, row_index, row_weight, col_index, col_weight, assignment, target_image):
    slices, cells = density.shape[0], density.shape[1]
    views, flat = target_image.shape
    pixels = row_index.shape[1]
    wide, tiles = 2 * pixels, flat * views // (8 * 2 * pixels)
    chunks = tiles // nz
    share = slices // (2 * ny)
    lines = flat // 128
    groups = wide // 128
    units = chunks - 1 + groups
    vm = pl.BlockSpec(memory_space=pltpu.VMEM)
    dma = pltpu.SemaphoreType.DMA
    image, grad = pl.pallas_call(
        functools.partial(kernel, (nx, nz, ny, slices * nx * nz)),
        out_shape=(
            jax.ShapeDtypeStruct((views * lines, 128), F32),
            jax.ShapeDtypeStruct((share, cells, cells), F32),
        ),
        in_specs=[pl.BlockSpec(memory_space=pltpu.HBM)] * 7,
        out_specs=(vm, vm),
        scratch_shapes=[
            pltpu.SMEM(assignment.shape, jnp.int32),
            pltpu.VMEM(density.shape, BF),
            pltpu.VMEM(row_index.shape, jnp.int32),
            pltpu.VMEM(row_index.shape, F32),
            pltpu.VMEM(row_index.shape, jnp.int32),
            pltpu.VMEM(row_index.shape, F32),
            pltpu.VMEM((views * lines, 128), F32),
            dma((7,)),
            pltpu.VMEM((8, wide), jnp.int32),
            pltpu.VMEM((8, wide), F32),
            pltpu.VMEM((2, 2 * cells, cells), F32),
            pltpu.VMEM((wide, cells), BF),
            pltpu.VMEM((chunks, cells, 16 * nz), BF),
            pltpu.VMEM((2, 2 * cells, wide), BF),
            pltpu.VMEM((2, wide, 2 * cells), BF),
            pltpu.VMEM((slices, 8 * nz, 2 * cells), BF),
            pltpu.VMEM((slices, pixels, wide), F32),
            pltpu.VMEM((pixels, wide), F32),
            pltpu.VMEM((pixels, wide), F32),
            pltpu.VMEM((pixels, wide), F32),
            pltpu.VMEM((tiles, groups, 2, 8, 128), F32),
            pltpu.VMEM((chunks, nz, groups, 2, 8, 128), F32),
            pltpu.VMEM((chunks, nz, groups, 8, 128), F32),
            pltpu.VMEM((chunks, groups, 2, 8, 128), F32),
            pltpu.VMEM((chunks, nx, groups, 2, 8, 128), F32),
            pltpu.VMEM((chunks, nz, groups, 8, 128), F32),
            pltpu.VMEM((tiles, groups, 8, 128), F32),
            pltpu.VMEM((groups, tiles, 8, 128), F32),
            pltpu.VMEM((slices, cells, cells), F32),
            pltpu.VMEM((ny, 2 * share, cells, cells), F32),
            pltpu.VMEM((ny, share, cells, cells), F32),
            pltpu.VMEM((ny, share, cells, cells), F32),
            pltpu.VMEM((ny, share, cells, cells), F32),
            pltpu.VMEM((2, share // 2, cells, cells), F32),
            pltpu.VMEM((2, share // 2, cells, cells), F32),
            pltpu.VMEM((cells // (2 * ny), cells), F32),
            pltpu.VMEM((nz, cells // (2 * ny), cells), F32),
            pltpu.VMEM((cells // (2 * ny), cells), F32),
            pltpu.VMEM((nx, cells // (2 * ny), cells), F32),
            pltpu.VMEM((2 * ny, cells // (2 * ny), cells), F32),
            pltpu.VMEM((pixels, wide), F32),
            dma((units, nz)), dma((units, nz)),
            dma((units, nx)), dma((units, nx)),
            dma((units, nz)), dma((units, nz)),
            dma((ny,)), dma((ny,)),
            dma((ny, 2)), dma((ny, 2)),
            dma((chunks, groups, nz)), dma((chunks, groups, nz)),
            dma((chunks, groups, nx)), dma((chunks, groups)),
            dma((nz,)), dma((nz,)),
            dma((nx,)), dma((nx,)),
            dma((2 * ny,)), dma((2 * ny,)),
            dma((2,)), dma((2,)),
        ],
        compiler_params=pltpu.CompilerParams(
            collective_id=0, has_side_effects=True, vmem_limit_bytes=50331648
        ),
    )(*[pltpu.with_memory_space_constraint(a, pltpu.HBM) for a in (
        assignment, density, row_index, row_weight, col_index, col_weight,
        target_image.reshape(views, lines, 128).transpose(1, 0, 2).reshape(views * lines, 128),
    )])
    return image.reshape(lines, views, 128).transpose(1, 0, 2).reshape(views, flat), grad


def solution(mesh, nz=ZDEV):
    placed = (P("depth", None, None), P(), P(), P(), P(), P("views"), P("views", None))
    nx, ny = mesh.shape["depth"] // nz, mesh.shape["views"] // 2
    return jax.shard_map(
        functools.partial(on_device, nx, nz, ny),
        mesh=mesh,
        in_specs=placed,
        out_specs=(P("views", None), P(("depth", "views"), None, None)),
        check_vma=False,
    )
```

```python
import functools

import jax
import jax.numpy as jnp
from jax import lax
from jax.experimental import pallas as pl
from jax.experimental.pallas import tpu as pltpu
from jax.sharding import PartitionSpec as P

MESH = pl.DeviceIdType.MESH
ZDEV = 8
BF = jnp.bfloat16
F32 = jnp.float32
LOG2E = 1.4426950408889634


def spread_order(n):
    out = []
    for k in range(1, n // 2 + 1):
        for o in (k, n - k):
            if o not in out and 0 < o < n:
                out.append(o)
    return out


def kernel(
    dims, *refs
):
    (
    assign_h, density_h, row_index_h, row_weight_h, col_index_h, col_weight_h, target_h, image, grad,
    assign, density, row_index, row_weight, col_index, col_weight, target, loads,
    pad_i, pad_w, tall, rows_m, rows_t, cols_m, cols_t, crossed, work, goal, gain, shift,
    mine, theirs, local, slab, slabs, back, final, totals, part, ended, got, summed, pieces, relay, passed,
    mass, masses, slab_mass, slab_masses, before, ahead,
    s1, r1, s2, r2, s3, r3, s4, r4, s5, r5, s6, r6, s7, r7, s8, r8, s9, r9, s10, r10, s11, r11,
    ) = refs
    nx, nz, ny, levels = dims
    step = 1.5 / levels
    slices, cells = density.shape[0], density.shape[1]
    half = row_index.shape[1] // 2
    pixels = 2 * half
    wide = 2 * pixels
    chunks = 2 * half // 8 // nz
    share = slices // (2 * ny)
    groups = wide // 128
    last = chunks - 1
    units = [(k, slice(0, groups)) for k in range(last)] + [(last, slice(0, 2)), (last, slice(2, groups))]
    depth, vw = lax.axis_index("depth"), lax.axis_index("views")
    x, z = depth // nz, depth % nz
    y, core = vw // 2, vw % 2

    def at_z(q):
        return (x * nz + q, vw)

    def at_x(q):
        return (q * nz + z, vw)

    def at_y(q):
        return (depth, q * 2 + core)

    partner = (depth, y * 2 + 1 - core)
    beside = spread_order(2 * ny)
    rows_held = cells // (2 * ny)
    z_off, x_off, y_off = (spread_order(n)[::-1] for n in (nz, nx, ny))

    fetch = [
        pltpu.make_async_copy(src, dst, loads.at[n])
        for n, (src, dst) in enumerate(
            [
                (assign_h, assign), (row_index_h, row_index), (row_weight_h, row_weight),
                (col_index_h, col_index), (col_weight_h, col_weight),
                (density_h, density), (target_h, target),
            ]
        )
    ]
    for copy in fetch:
        copy.start()

    barrier = pltpu.get_barrier_semaphore()
    for o in z_off:
        pl.semaphore_signal(barrier, inc=1, device_id=at_z((z + o) % nz), device_id_type=MESH)
    for o in x_off:
        pl.semaphore_signal(barrier, inc=1, device_id=at_x((x + o) % nx), device_id_type=MESH)
    for o in beside:
        pl.semaphore_signal(barrier, inc=1, device_id=(depth, (vw + o) % (2 * ny)), device_id_type=MESH)

    for copy in fetch[:5]:
        copy.wait()
    pad_i[...] = jnp.full(pad_i.shape, -2, jnp.int32)
    pad_w[...] = jnp.zeros(pad_w.shape, F32)
    for v in range(2):
        a = assign[v]
        pad_i[v : v + 1, 0:pixels] = row_index[pl.ds(a, 1), :]
        pad_w[v : v + 1, 0:pixels] = row_weight[pl.ds(a, 1), :]
        pad_i[2 + v : 3 + v, 0:pixels] = col_index[pl.ds(a, 1), :]
        pad_w[2 + v : 3 + v, 0:pixels] = col_weight[pl.ds(a, 1), :]

    def resampler(row, lanes):
        idx, w = pad_i[row : row + 1, 0:lanes], pad_w[row : row + 1, 0:lanes]
        places = lax.broadcasted_iota(jnp.int32, (cells, lanes), 0)
        zero = jnp.zeros((cells, lanes), F32)
        return jnp.where(places == idx, 1.0 - w, zero) + jnp.where(places == idx + 1, w, zero)

    tall_rows = 8 * nz

    def resamplers(v):
        tall[v] = resampler(v, 2 * cells).T
        for p in range(2):
            rows_m[p * pixels + v * half : p * pixels + (v + 1) * half, :] = tall[
                v, pl.ds(p, half, stride=2), :
            ].astype(BF)
        ct = resampler(2 + v, wide)
        cols_m[v] = jnp.concatenate([ct, pltpu.roll(ct, pixels, 1)], axis=0).astype(BF)

    def transposed():
        for v in range(2):
            cols_t[v] = cols_m[v].T
        for k in range(chunks):
            at = k * tall_rows
            rows_t[k] = jnp.concatenate(
                [rows_m[p * pixels + at : p * pixels + at + tall_rows, :] for p in range(2)], axis=0
            ).T

    def views_in(k):
        out = []
        for v in range(2):
            lo, hi = max(k * tall_rows, v * half), min((k + 1) * tall_rows, (v + 1) * half)
            if lo < hi:
                out.append((v, lo - k * tall_rows, hi - lo))
        return out

    def sample(k):
        at = k * tall_rows
        lhs = jnp.concatenate(
            [rows_m[p * pixels + at : p * pixels + at + tall_rows, :] for p in range(2)], axis=0
        )
        for pair in range(slices // 2):
            two = jnp.concatenate([density[2 * pair], density[2 * pair + 1]], axis=1)
            out = jnp.dot(lhs, two, preferred_element_type=F32).astype(BF)
            for s in range(2):
                cut = out[:, s * cells : (s + 1) * cells]
                crossed[2 * pair + s] = jnp.concatenate([cut[:tall_rows], cut[tall_rows:]], axis=1)
        for v, first, n in views_in(k):
            out = jnp.dot(
                crossed[:, first : first + n, :].reshape(slices * n, 2 * cells),
                cols_m[v],
                preferred_element_type=F32,
            )
            work[:, at + first : at + first + n, :] = out.reshape(slices, n, wide)

    def march(tile):
        at = pl.ds(pl.multiple_of(tile * 8, 8), 8)
        through = jnp.ones((8, wide), F32)
        inclusive = jnp.zeros((8, wide), F32)
        for s in range(slices):
            value = work[s, at, :]
            optical = step * value
            att = jnp.exp2(value * (-step * LOG2E))
            gone = 1.0 - att
            inclusive = inclusive + through * (optical * gone)
            work[s, at, :] = through * (gone + optical * att) + inclusive
            through = through * att
        for g in range(groups):
            lanes = slice(g * 128, (g + 1) * 128)
            mine[tile, g, 0] = inclusive[:, lanes] * (1.0 / step)
            mine[tile, g, 1] = through[:, lanes]

    pending = []

    def send(src, dst, ssem, rsem, device):
        copy = pltpu.make_async_remote_copy(
            src_ref=src, dst_ref=dst, send_sem=ssem, recv_sem=rsem, device_id=device, device_id_type=MESH
        )
        copy.start()
        return copy

    def arrived(dst, rsem):
        pltpu.make_async_remote_copy(
            src_ref=dst, dst_ref=dst, send_sem=rsem, recv_sem=rsem, device_id=partner, device_id_type=MESH
        ).wait_recv()

    def mass_sent():
        held = density[:, pl.ds(pl.multiple_of(vw * rows_held, rows_held), rows_held), :]
        one = jnp.sum(held.astype(F32), axis=0)
        mass[...] = one
        masses[z] = one
        for o in z_off:
            q = (z + o) % nz
            pending.append(send(mass, masses.at[z], s8.at[q], r8.at[z], at_z(q)))

    def mass_along_z():
        for o in z_off:
            q = (z + o) % nz
            arrived(masses.at[q], r8.at[q])
        lead = jnp.zeros((rows_held, cells), F32)
        total = lead
        for q in range(nz):
            lead = jnp.where(q == z, total, lead)
            total = total + masses[q]
        slab_mass[...] = total
        before[vw] = lead
        for o in x_off:
            q = (x + o) % nx
            pending.append(send(slab_mass, slab_masses.at[x], s9.at[q], r9.at[x], at_x(q)))

    def mass_along_x():
        slab_masses[x] = jnp.zeros((rows_held, cells), F32)
        for o in x_off:
            q = (x + o) % nx
            arrived(slab_masses.at[q], r9.at[q])
        lead = before[vw]
        for q in range(nx):
            lead = lead + jnp.where(q < x, slab_masses[q], 0.0)
        before[vw] = lead
        for o in beside:
            q = (vw + o) % (2 * ny)
            pending.append(send(before.at[vw], before.at[vw], s10.at[q], r10.at[vw], (depth, q)))

    def split(value):
        high = value.astype(BF)
        return high, (value - high.astype(F32)).astype(BF)

    def see_ahead():
        for o in beside:
            q = (vw + o) % (2 * ny)
            arrived(before.at[q], r10.at[q])
        two = jnp.concatenate(split(before[...].reshape(cells, cells)), axis=1)
        out = jnp.dot(rows_m[...], two, preferred_element_type=F32)
        out = out[:, :cells] + out[:, cells:]
        parts = split(jnp.concatenate([out[:pixels], out[pixels:]], axis=1))
        for v in range(2):
            at = slice(v * half, (v + 1) * half)
            passed = sum(jnp.dot(part[at], cols_m[v], preferred_element_type=F32) for part in parts)
            ahead[at] = jnp.exp2(passed * (-step * LOG2E))

    def send_share(u, q):
        k, gs = units[u]
        pending.append(
            send(mine.at[k * nz + q, gs], theirs.at[k, z, gs], s1.at[u, q], r1.at[u, z], at_z(q))
        )

    built = 0
    for k in range(chunks):
        for v, _, _ in views_in(k):
            if v >= built:
                resamplers(v)
                built = v + 1
        if k == 0:
            fetch[5].wait()
        sample(k)
        for q in range(nz):
            march(k * nz + q)
        if k == 0:
            pl.semaphore_wait(barrier, len(z_off) + len(x_off) + len(beside))
        for u in [k] if k < last else range(last, len(units)):
            for o in z_off:
                send_share(u, (z + o) % nz)
        if k == 0:
            mass_sent()
    transposed()

    fetch[6].wait()
    for v in range(2):
        for g in range(groups):
            goal[v * half : (v + 1) * half, g * 128 : (g + 1) * 128] = target[
                pl.ds(2 * g + v, half, stride=2 * groups), :
            ]

    def slab_of(u):
        k, gs = units[u]
        theirs[k, z, gs] = mine[k * nz + z, gs]
        for o in z_off:
            q = (z + o) % nz
            arrived(theirs.at[k, q, gs], r1.at[u, q])
        c = jnp.zeros((gs.stop - gs.start, 8, 128), F32)
        t = jnp.ones((gs.stop - gs.start, 8, 128), F32)
        for q in range(nz):
            local[k, q, gs] = c
            c = c + t * theirs[k, q, gs, 0]
            t = t * theirs[k, q, gs, 1]
        slab[k, gs, 0] = c
        slab[k, gs, 1] = t
        slabs[k, x, gs, 0] = c
        slabs[k, x, gs, 1] = t
        for o in x_off:
            q = (x + o) % nx
            pending.append(send(slab.at[k, gs], slabs.at[k, x, gs], s2.at[u, q], r2.at[u, x], at_x(q)))

    def lead_of(u):
        k, gs = units[u]
        for o in x_off:
            q = (x + o) % nx
            arrived(slabs.at[k, q, gs], r2.at[u, q])
        lead_c = jnp.zeros((gs.stop - gs.start, 8, 128), F32)
        lead_t = jnp.ones((gs.stop - gs.start, 8, 128), F32)
        c, t = lead_c, lead_t
        for q in range(nx):
            c = c + t * slabs[k, q, gs, 0]
            t = t * slabs[k, q, gs, 1]
            earlier = q < x
            lead_c = jnp.where(earlier, c, lead_c)
            lead_t = jnp.where(earlier, t, lead_t)
        own = k * nz + z
        if k == last:
            for g in range(gs.start, gs.stop):
                totals[g, own] = c[g - gs.start]
            for o in z_off:
                q = (z + o) % nz
                for g in range(gs.start, gs.stop):
                    one = totals.at[g, own]
                    pending.append(send(one, one, s6.at[k, g, q], r6.at[k, g, z], at_z(q)))
        else:
            for g in range(groups):

                @pl.when(x == g % nx)
                def _():
                    totals[g, own] = c[g]
                    for o in z_off:
                        q = (z + o) % nz
                        send(totals.at[g, own], totals.at[g, own], s6.at[k, g, q], r6.at[k, g, z], at_z(q))

        for q in range(nz):
            back[k, q, gs] = c - (lead_c + lead_t * local[k, q, gs])
        for o in z_off:
            q = (z + o) % nz
            pending.append(send(back.at[k, q, gs], final.at[own, gs], s3.at[u, q], r3.at[u, z], at_z(q)))
        final[own, gs] = back[k, z, gs]

    def share_of(k):
        for g in range(groups):

            @pl.when(x == g % nx)
            def _():
                for o in z_off:
                    q = (z + o) % nz
                    arrived(totals.at[g, k * nz + q], r6.at[k, g, q])
                for o in x_off:
                    q = (x + o) % nx
                    tiles = totals.at[g, k * nz : (k + 1) * nz]
                    send(tiles, tiles, s7.at[k, g, q], r7.at[k, g], at_x(q))

    def sent_totals(k):
        for g in range(groups):

            @pl.when(x == g % nx)
            def _():
                one = totals.at[g, k * nz + z]
                tiles = totals.at[g, k * nz : (k + 1) * nz]
                for o in z_off:
                    q = (z + o) % nz
                    pltpu.make_async_remote_copy(
                        src_ref=one, dst_ref=one, send_sem=s6.at[k, g, q], recv_sem=r6.at[k, g, z],
                        device_id=at_z(q), device_id_type=MESH,
                    ).wait_send()
                for o in x_off:
                    q = (x + o) % nx
                    pltpu.make_async_remote_copy(
                        src_ref=tiles, dst_ref=tiles, send_sem=s7.at[k, g, q], recv_sem=r7.at[k, g],
                        device_id=at_x(q), device_id_type=MESH,
                    ).wait_send()

    def weigh(k):
        for u, (j, gs) in enumerate(units):
            if j == k:
                for o in z_off:
                    q = (z + o) % nz
                    arrived(final.at[k * nz + q, gs], r3.at[u, q])
        for g in range(groups):
            if k == last:
                for o in z_off:
                    q = (z + o) % nz
                    arrived(totals.at[g, k * nz + q], r6.at[k, g, q])
            else:

                @pl.when(x != g % nx)
                def _():
                    arrived(totals.at[g, k * nz : (k + 1) * nz], r7.at[k, g])

        at = slice(k * tall_rows, (k + 1) * tall_rows)
        tiles = slice(k * nz, (k + 1) * nz)
        total = jnp.concatenate([totals[g, tiles].reshape(tall_rows, 128) for g in range(groups)], axis=1)
        residue = levels * (total - goal[at])
        gain[at] = residue * ahead[at]
        behind = jnp.concatenate([final[tiles, g].reshape(tall_rows, 128) for g in range(groups)], axis=1)
        shift[at] = step * residue * behind

    def terms(k, first, count):
        at = slice(k * tall_rows, (k + 1) * tall_rows)
        g = [(gain[at] * work[first + s, at] - shift[at]).astype(BF) for s in range(count)]
        spread = [
            (
                n,
                jnp.dot(
                    jnp.concatenate([g[s][a : a + n] for s in range(count)], axis=0),
                    cols_t[v],
                    preferred_element_type=F32,
                ).astype(BF),
            )
            for v, a, n in views_in(k)
        ]
        out = []
        for pair in range(0, count, 2):
            stack = jnp.concatenate(
                [
                    jnp.concatenate(
                        [
                            value[s * n : (s + 1) * n, p * cells : (p + 1) * cells]
                            for p in range(2)
                            for n, value in spread
                        ],
                        axis=0,
                    )
                    for s in (pair, pair + 1)
                ],
                axis=1,
            )
            both = jnp.dot(rows_t[k], stack, preferred_element_type=F32)
            out += [both[:, :cells], both[:, cells:]]
        return out

    def collect(k):
        def body(i, carry):
            for s, value in enumerate(terms(k, 4 * i, 4)):
                part[4 * i + s] = value if k == 0 else part[4 * i + s] + value
            return carry

        lax.fori_loop(0, slices // 4, body, 0)

    slab_of(0)
    mass_along_z()
    lead_of(0)
    mass_along_x()
    for k in range(1, last):
        slab_of(k)
        if k == last - 1:
            slab_of(last)
        lead_of(k)
        share_of(k - 1)
    see_ahead()
    for u in range(last + 1, len(units)):
        slab_of(u)
    for u in range(last, len(units)):
        lead_of(u)
    share_of(last - 1)
    for k in range(last):
        weigh(k)
        collect(k)
    weigh(last)

    up, down = (y + 1) % ny, (y + ny - 1) % ny
    halves = slice(0, share // 2), slice(share // 2, share)

    def give_half(n, src, q):
        pending.append(send(src, pieces.at[y, halves[n]], s5.at[q, n], r5.at[y, n], at_y(q)))

    def merge(o):
        q = (y + o) % ny
        arrived(got.at[q], r4.at[q])
        summed[q] = ended[q, pl.ds(core * share, share)] + got[q]
        if o == 2:
            for n, near in enumerate((up, down)):
                pending.append(send(summed.at[q, halves[n]], relay.at[n], s11.at[n], r11.at[n], at_y(near)))
        elif o == 1:
            give_half(1, summed.at[q, halves[1]], q)
        elif o == 3:
            give_half(0, summed.at[q, halves[0]], q)

    def pass_on():
        for n, near in enumerate((up, down)):
            arrived(relay.at[n], r11.at[n])
            passed[n] = summed[near, halves[n]] + relay[n]
            give_half(n, passed.at[n], near)

    order = y_off + [0]
    for n, o in enumerate(order):
        q = (y + o) % ny
        first = 2 * q * share
        for s, value in enumerate(terms(last, first, 2 * share)):
            ended[q, s] = part[first + s] + value
        pending.append(
            send(ended.at[q, pl.ds((1 - core) * share, share)], got.at[q], s4.at[q], r4.at[q], partner)
        )
        if n:
            merge(order[n - 1])
    merge(0)
    pass_on()

    per = half // 8
    for v in range(2):
        for g in range(groups):
            image[pl.ds(2 * g + v, half, stride=2 * groups), :] = totals[
                g, v * per : (v + 1) * per
            ].reshape(half, 128)

    total = summed[y]
    for q in (down, up):
        for n in range(2):
            arrived(pieces.at[q, halves[n]], r5.at[q, n])
        total = total + pieces[q]
    grad[...] = total
    for copy in pending:
        copy.wait_send()
    for k in range(last):
        sent_totals(k)


def write_out(image, grad, image_out, grad_out, sems):
    copies = [
        pltpu.make_async_copy(src, dst, sems.at[n])
        for n, (src, dst) in enumerate(((image, image_out), (grad, grad_out)))
    ]
    for copy in copies:
        copy.start()
    for copy in copies:
        copy.wait()


def on_device(nx, nz, ny, density, row_index, row_weight, col_index, col_weight, assignment, target_image):
    slices, cells = density.shape[0], density.shape[1]
    views, flat = target_image.shape
    pixels = row_index.shape[1]
    wide, tiles = 2 * pixels, flat * views // (8 * 2 * pixels)
    chunks = tiles // nz
    share = slices // (2 * ny)
    lines = flat // 128
    groups = wide // 128
    units = chunks - 1 + groups
    vm = pl.BlockSpec(memory_space=pltpu.VMEM)
    dma = pltpu.SemaphoreType.DMA
    image, grad = pl.pallas_call(
        functools.partial(kernel, (nx, nz, ny, slices * nx * nz)),
        out_shape=(
            jax.ShapeDtypeStruct((views * lines, 128), F32),
            jax.ShapeDtypeStruct((share, cells, cells), F32),
        ),
        in_specs=[pl.BlockSpec(memory_space=pltpu.HBM)] * 7,
        out_specs=(vm, vm),
        scratch_shapes=[
            pltpu.SMEM(assignment.shape, jnp.int32),
            pltpu.VMEM(density.shape, BF),
            pltpu.VMEM(row_index.shape, jnp.int32),
            pltpu.VMEM(row_index.shape, F32),
            pltpu.VMEM(row_index.shape, jnp.int32),
            pltpu.VMEM(row_index.shape, F32),
            pltpu.VMEM((views * lines, 128), F32),
            dma((7,)),
            pltpu.VMEM((8, wide), jnp.int32),
            pltpu.VMEM((8, wide), F32),
            pltpu.VMEM((2, 2 * cells, cells), F32),
            pltpu.VMEM((wide, cells), BF),
            pltpu.VMEM((chunks, cells, 16 * nz), BF),
            pltpu.VMEM((2, 2 * cells, wide), BF),
            pltpu.VMEM((2, wide, 2 * cells), BF),
            pltpu.VMEM((slices, 8 * nz, 2 * cells), BF),
            pltpu.VMEM((slices, pixels, wide), F32),
            pltpu.VMEM((pixels, wide), F32),
            pltpu.VMEM((pixels, wide), F32),
            pltpu.VMEM((pixels, wide), F32),
            pltpu.VMEM((tiles, groups, 2, 8, 128), F32),
            pltpu.VMEM((chunks, nz, groups, 2, 8, 128), F32),
            pltpu.VMEM((chunks, nz, groups, 8, 128), F32),
            pltpu.VMEM((chunks, groups, 2, 8, 128), F32),
            pltpu.VMEM((chunks, nx, groups, 2, 8, 128), F32),
            pltpu.VMEM((chunks, nz, groups, 8, 128), F32),
            pltpu.VMEM((tiles, groups, 8, 128), F32),
            pltpu.VMEM((groups, tiles, 8, 128), F32),
            pltpu.VMEM((slices, cells, cells), F32),
            pltpu.VMEM((ny, 2 * share, cells, cells), F32),
            pltpu.VMEM((ny, share, cells, cells), F32),
            pltpu.VMEM((ny, share, cells, cells), F32),
            pltpu.VMEM((ny, share, cells, cells), F32),
            pltpu.VMEM((2, share // 2, cells, cells), F32),
            pltpu.VMEM((2, share // 2, cells, cells), F32),
            pltpu.VMEM((cells // (2 * ny), cells), F32),
            pltpu.VMEM((nz, cells // (2 * ny), cells), F32),
            pltpu.VMEM((cells // (2 * ny), cells), F32),
            pltpu.VMEM((nx, cells // (2 * ny), cells), F32),
            pltpu.VMEM((2 * ny, cells // (2 * ny), cells), F32),
            pltpu.VMEM((pixels, wide), F32),
            dma((units, nz)), dma((units, nz)),
            dma((units, nx)), dma((units, nx)),
            dma((units, nz)), dma((units, nz)),
            dma((ny,)), dma((ny,)),
            dma((ny, 2)), dma((ny, 2)),
            dma((chunks, groups, nz)), dma((chunks, groups, nz)),
            dma((chunks, groups, nx)), dma((chunks, groups)),
            dma((nz,)), dma((nz,)),
            dma((nx,)), dma((nx,)),
            dma((2 * ny,)), dma((2 * ny,)),
            dma((2,)), dma((2,)),
        ],
        compiler_params=pltpu.CompilerParams(
            collective_id=0, has_side_effects=True, vmem_limit_bytes=50331648
        ),
    )(*[pltpu.with_memory_space_constraint(a, pltpu.HBM) for a in (
        assignment, density, row_index, row_weight, col_index, col_weight,
        target_image.reshape(views, lines, 128).transpose(1, 0, 2).reshape(views * lines, 128),
    )])
    image, grad = pl.pallas_call(
        write_out,
        out_shape=(
            jax.ShapeDtypeStruct(image.shape, F32),
            jax.ShapeDtypeStruct(grad.shape, F32),
        ),
        in_specs=[vm, vm],
        out_specs=(pl.BlockSpec(memory_space=pltpu.HBM),) * 2,
        scratch_shapes=[dma((2,))],
        compiler_params=pltpu.CompilerParams(vmem_limit_bytes=1 << 20),
    )(image, grad)
    return image.reshape(lines, views, 128).transpose(1, 0, 2).reshape(views, flat), grad


def solution(mesh, nz=ZDEV):
    placed = (P("depth", None, None), P(), P(), P(), P(), P("views"), P("views", None))
    nx, ny = mesh.shape["depth"] // nz, mesh.shape["views"] // 2
    return jax.shard_map(
        functools.partial(on_device, nx, nz, ny),
        mesh=mesh,
        in_specs=placed,
        out_specs=(P("views", None), P(("depth", "views"), None, None)),
        check_vma=False,
    )
```

```python
import functools

import jax
import jax.numpy as jnp
from jax import lax
from jax.experimental import pallas as pl
from jax.experimental.pallas import tpu as pltpu
from jax.sharding import PartitionSpec as P

MESH = pl.DeviceIdType.MESH
ZDEV = 8
BF = jnp.bfloat16
F32 = jnp.float32
LOG2E = 1.4426950408889634


def spread_order(n):
    out = []
    for k in range(1, n // 2 + 1):
        for o in (k, n - k):
            if o not in out and 0 < o < n:
                out.append(o)
    return out


def kernel(
    dims, *refs
):
    (
    assign_h, density_h, row_index_h, row_weight_h, col_index_h, col_weight_h, target_h, image, grad,
    assign, density, row_index, row_weight, col_index, col_weight, target, loads,
    pad_i, pad_w, tall, rows_m, rows_t, cols_m, cols_t, crossed, work, goal, gain, shift,
    mine, theirs, local, slab, slabs, back, final, part, ended, got, summed, pieces, relay, passed,
    mass, masses, slab_mass, slab_masses, before, ahead,
    s1, r1, s2, r2, s3, r3, s4, r4, s5, r5, s8, r8, s9, r9, s10, r10, s11, r11,
    ) = refs
    nx, nz, ny, levels = dims
    step = 1.5 / levels
    slices, cells = density.shape[0], density.shape[1]
    half = row_index.shape[1] // 2
    pixels = 2 * half
    wide = 2 * pixels
    chunks = 2 * half // 8 // nz
    share = slices // (2 * ny)
    groups = wide // 128
    last = chunks - 1
    units = [(k, slice(0, groups)) for k in range(last)] + [(last, slice(0, 2)), (last, slice(2, groups))]
    depth, vw = lax.axis_index("depth"), lax.axis_index("views")
    x, z = depth // nz, depth % nz
    y, core = vw // 2, vw % 2

    def at_z(q):
        return (x * nz + q, vw)

    def at_x(q):
        return (q * nz + z, vw)

    def at_y(q):
        return (depth, q * 2 + core)

    partner = (depth, y * 2 + 1 - core)
    beside = spread_order(2 * ny)
    rows_held = cells // (2 * ny)
    z_off, x_off, y_off = (spread_order(n)[::-1] for n in (nz, nx, ny))

    fetch = [
        pltpu.make_async_copy(src, dst, loads.at[n])
        for n, (src, dst) in enumerate(
            [
                (assign_h, assign), (row_index_h, row_index), (row_weight_h, row_weight),
                (col_index_h, col_index), (col_weight_h, col_weight),
                (density_h, density), (target_h, target),
            ]
        )
    ]
    for copy in fetch:
        copy.start()

    barrier = pltpu.get_barrier_semaphore()
    for o in z_off:
        pl.semaphore_signal(barrier, inc=1, device_id=at_z((z + o) % nz), device_id_type=MESH)
    for o in x_off:
        pl.semaphore_signal(barrier, inc=1, device_id=at_x((x + o) % nx), device_id_type=MESH)
    for o in beside:
        pl.semaphore_signal(barrier, inc=1, device_id=(depth, (vw + o) % (2 * ny)), device_id_type=MESH)

    for copy in fetch[:5]:
        copy.wait()
    pad_i[...] = jnp.full(pad_i.shape, -2, jnp.int32)
    pad_w[...] = jnp.zeros(pad_w.shape, F32)
    for v in range(2):
        a = assign[v]
        pad_i[v : v + 1, 0:pixels] = row_index[pl.ds(a, 1), :]
        pad_w[v : v + 1, 0:pixels] = row_weight[pl.ds(a, 1), :]
        pad_i[2 + v : 3 + v, 0:pixels] = col_index[pl.ds(a, 1), :]
        pad_w[2 + v : 3 + v, 0:pixels] = col_weight[pl.ds(a, 1), :]

    def resampler(row, lanes):
        idx, w = pad_i[row : row + 1, 0:lanes], pad_w[row : row + 1, 0:lanes]
        places = lax.broadcasted_iota(jnp.int32, (cells, lanes), 0)
        zero = jnp.zeros((cells, lanes), F32)
        return jnp.where(places == idx, 1.0 - w, zero) + jnp.where(places == idx + 1, w, zero)

    tall_rows = 8 * nz

    def resamplers(v):
        tall[v] = resampler(v, 2 * cells).T
        for p in range(2):
            rows_m[p * pixels + v * half : p * pixels + (v + 1) * half, :] = tall[
                v, pl.ds(p, half, stride=2), :
            ].astype(BF)
        ct = resampler(2 + v, wide)
        cols_m[v] = jnp.concatenate([ct, pltpu.roll(ct, pixels, 1)], axis=0).astype(BF)

    def transposed():
        for v in range(2):
            cols_t[v] = cols_m[v].T
        for k in range(chunks):
            at = k * tall_rows
            rows_t[k] = jnp.concatenate(
                [rows_m[p * pixels + at : p * pixels + at + tall_rows, :] for p in range(2)], axis=0
            ).T

    def views_in(k):
        out = []
        for v in range(2):
            lo, hi = max(k * tall_rows, v * half), min((k + 1) * tall_rows, (v + 1) * half)
            if lo < hi:
                out.append((v, lo - k * tall_rows, hi - lo))
        return out

    def sample(k):
        at = k * tall_rows
        lhs = jnp.concatenate(
            [rows_m[p * pixels + at : p * pixels + at + tall_rows, :] for p in range(2)], axis=0
        )
        for pair in range(slices // 2):
            two = jnp.concatenate([density[2 * pair], density[2 * pair + 1]], axis=1)
            out = jnp.dot(lhs, two, preferred_element_type=F32).astype(BF)
            for s in range(2):
                cut = out[:, s * cells : (s + 1) * cells]
                crossed[2 * pair + s] = jnp.concatenate([cut[:tall_rows], cut[tall_rows:]], axis=1)
        for v, first, n in views_in(k):
            out = jnp.dot(
                crossed[:, first : first + n, :].reshape(slices * n, 2 * cells),
                cols_m[v],
                preferred_element_type=F32,
            )
            work[:, at + first : at + first + n, :] = out.reshape(slices, n, wide)

    def march(tile):
        at = pl.ds(pl.multiple_of(tile * 8, 8), 8)
        through = jnp.ones((8, wide), F32)
        inclusive = jnp.zeros((8, wide), F32)
        for s in range(slices):
            value = work[s, at, :]
            optical = step * value
            att = jnp.exp2(value * (-step * LOG2E))
            gone = 1.0 - att
            inclusive = inclusive + through * (optical * gone)
            work[s, at, :] = through * (gone + optical * att) + inclusive
            through = through * att
        for g in range(groups):
            lanes = slice(g * 128, (g + 1) * 128)
            mine[tile, g, 0] = inclusive[:, lanes] * (1.0 / step)
            mine[tile, g, 1] = through[:, lanes]

    pending = []

    def send(src, dst, ssem, rsem, device):
        copy = pltpu.make_async_remote_copy(
            src_ref=src, dst_ref=dst, send_sem=ssem, recv_sem=rsem, device_id=device, device_id_type=MESH
        )
        copy.start()
        return copy

    def arrived(dst, rsem):
        pltpu.make_async_remote_copy(
            src_ref=dst, dst_ref=dst, send_sem=rsem, recv_sem=rsem, device_id=partner, device_id_type=MESH
        ).wait_recv()

    def mass_sent():
        held = density[:, pl.ds(pl.multiple_of(vw * rows_held, rows_held), rows_held), :]
        one = jnp.sum(held.astype(F32), axis=0)
        mass[...] = one
        masses[z] = one
        for o in z_off:
            q = (z + o) % nz
            pending.append(send(mass, masses.at[z], s8.at[q], r8.at[z], at_z(q)))

    def mass_along_z():
        for o in z_off:
            q = (z + o) % nz
            arrived(masses.at[q], r8.at[q])
        lead = jnp.zeros((rows_held, cells), F32)
        total = lead
        for q in range(nz):
            lead = jnp.where(q == z, total, lead)
            total = total + masses[q]
        slab_mass[...] = total
        before[vw] = lead
        for o in x_off:
            q = (x + o) % nx
            pending.append(send(slab_mass, slab_masses.at[x], s9.at[q], r9.at[x], at_x(q)))

    def mass_along_x():
        slab_masses[x] = jnp.zeros((rows_held, cells), F32)
        for o in x_off:
            q = (x + o) % nx
            arrived(slab_masses.at[q], r9.at[q])
        lead = before[vw]
        for q in range(nx):
            lead = lead + jnp.where(q < x, slab_masses[q], 0.0)
        before[vw] = lead
        for o in beside:
            q = (vw + o) % (2 * ny)
            pending.append(send(before.at[vw], before.at[vw], s10.at[q], r10.at[vw], (depth, q)))

    def split(value):
        high = value.astype(BF)
        return high, (value - high.astype(F32)).astype(BF)

    def see_ahead():
        for o in beside:
            q = (vw + o) % (2 * ny)
            arrived(before.at[q], r10.at[q])
        two = jnp.concatenate(split(before[...].reshape(cells, cells)), axis=1)
        out = jnp.dot(rows_m[...], two, preferred_element_type=F32)
        out = out[:, :cells] + out[:, cells:]
        parts = split(jnp.concatenate([out[:pixels], out[pixels:]], axis=1))
        for v in range(2):
            at = slice(v * half, (v + 1) * half)
            passed = sum(jnp.dot(part[at], cols_m[v], preferred_element_type=F32) for part in parts)
            ahead[at] = jnp.exp2(passed * (-step * LOG2E))

    def send_share(u, q):
        k, gs = units[u]
        pending.append(
            send(mine.at[k * nz + q, gs], theirs.at[k, z, gs], s1.at[u, q], r1.at[u, z], at_z(q))
        )

    built = 0
    for k in range(chunks):
        for v, _, _ in views_in(k):
            if v >= built:
                resamplers(v)
                built = v + 1
        if k == 0:
            fetch[5].wait()
        sample(k)
        for q in range(nz):
            march(k * nz + q)
        if k == 0:
            pl.semaphore_wait(barrier, len(z_off) + len(x_off) + len(beside))
        for u in [k] if k < last else range(last, len(units)):
            for o in z_off:
                send_share(u, (z + o) % nz)
        if k == 0:
            mass_sent()
    transposed()

    fetch[6].wait()
    for v in range(2):
        for g in range(groups):
            goal[v * half : (v + 1) * half, g * 128 : (g + 1) * 128] = target[
                pl.ds(2 * g + v, half, stride=2 * groups), :
            ]

    def slab_of(u):
        k, gs = units[u]
        theirs[k, z, gs] = mine[k * nz + z, gs]
        for o in z_off:
            q = (z + o) % nz
            arrived(theirs.at[k, q, gs], r1.at[u, q])
        c = jnp.zeros((gs.stop - gs.start, 8, 128), F32)
        t = jnp.ones((gs.stop - gs.start, 8, 128), F32)
        for q in range(nz):
            local[k, q, gs] = c
            c = c + t * theirs[k, q, gs, 0]
            t = t * theirs[k, q, gs, 1]
        slab[k, gs, 0] = c
        slab[k, gs, 1] = t
        slabs[k, x, gs, 0] = c
        slabs[k, x, gs, 1] = t
        for o in x_off:
            q = (x + o) % nx
            pending.append(send(slab.at[k, gs], slabs.at[k, x, gs], s2.at[u, q], r2.at[u, x], at_x(q)))

    def lead_of(u):
        k, gs = units[u]
        for o in x_off:
            q = (x + o) % nx
            arrived(slabs.at[k, q, gs], r2.at[u, q])
        lead_c = jnp.zeros((gs.stop - gs.start, 8, 128), F32)
        lead_t = jnp.ones((gs.stop - gs.start, 8, 128), F32)
        c, t = lead_c, lead_t
        for q in range(nx):
            c = c + t * slabs[k, q, gs, 0]
            t = t * slabs[k, q, gs, 1]
            earlier = q < x
            lead_c = jnp.where(earlier, c, lead_c)
            lead_t = jnp.where(earlier, t, lead_t)
        own = k * nz + z
        for q in range(nz):
            back[k, q, gs, 0] = c - (lead_c + lead_t * local[k, q, gs])
            back[k, q, gs, 1] = c
        for o in z_off:
            q = (z + o) % nz
            pending.append(send(back.at[k, q, gs], final.at[own, gs], s3.at[u, q], r3.at[u, z], at_z(q)))
        final[own, gs] = back[k, z, gs]

    def weigh(k):
        for u, (j, gs) in enumerate(units):
            if j == k:
                for o in z_off:
                    q = (z + o) % nz
                    arrived(final.at[k * nz + q, gs], r3.at[u, q])
        at = slice(k * tall_rows, (k + 1) * tall_rows)
        tiles = slice(k * nz, (k + 1) * nz)
        total = jnp.concatenate([final[tiles, g, 1].reshape(tall_rows, 128) for g in range(groups)], axis=1)
        residue = levels * (total - goal[at])
        gain[at] = residue * ahead[at]
        behind = jnp.concatenate([final[tiles, g, 0].reshape(tall_rows, 128) for g in range(groups)], axis=1)
        shift[at] = step * residue * behind

    def terms(k, first, count):
        at = slice(k * tall_rows, (k + 1) * tall_rows)
        g = [(gain[at] * work[first + s, at] - shift[at]).astype(BF) for s in range(count)]
        spread = [
            (
                n,
                jnp.dot(
                    jnp.concatenate([g[s][a : a + n] for s in range(count)], axis=0),
                    cols_t[v],
                    preferred_element_type=F32,
                ).astype(BF),
            )
            for v, a, n in views_in(k)
        ]
        out = []
        for pair in range(0, count, 2):
            stack = jnp.concatenate(
                [
                    jnp.concatenate(
                        [
                            value[s * n : (s + 1) * n, p * cells : (p + 1) * cells]
                            for p in range(2)
                            for n, value in spread
                        ],
                        axis=0,
                    )
                    for s in (pair, pair + 1)
                ],
                axis=1,
            )
            both = jnp.dot(rows_t[k], stack, preferred_element_type=F32)
            out += [both[:, :cells], both[:, cells:]]
        return out

    def collect(k):
        def body(i, carry):
            for s, value in enumerate(terms(k, 4 * i, 4)):
                part[4 * i + s] = value if k == 0 else part[4 * i + s] + value
            return carry

        lax.fori_loop(0, slices // 4, body, 0)

    slab_of(0)
    mass_along_z()
    lead_of(0)
    mass_along_x()
    for k in range(1, last):
        slab_of(k)
        if k == last - 1:
            slab_of(last)
        lead_of(k)
    see_ahead()
    for u in range(last + 1, len(units)):
        slab_of(u)
    for u in range(last, len(units)):
        lead_of(u)
    for k in range(last):
        weigh(k)
        collect(k)
    weigh(last)

    up, down = (y + 1) % ny, (y + ny - 1) % ny
    halves = slice(0, share // 2), slice(share // 2, share)

    def give_half(n, src, q):
        pending.append(send(src, pieces.at[y, halves[n]], s5.at[q, n], r5.at[y, n], at_y(q)))

    def merge(o):
        q = (y + o) % ny
        arrived(got.at[q], r4.at[q])
        summed[q] = ended[q, pl.ds(core * share, share)] + got[q]
        if o == 2:
            for n, near in enumerate((up, down)):
                pending.append(send(summed.at[q, halves[n]], relay.at[n], s11.at[n], r11.at[n], at_y(near)))
        elif o == 1:
            give_half(1, summed.at[q, halves[1]], q)
        elif o == 3:
            give_half(0, summed.at[q, halves[0]], q)

    def pass_on():
        for n, near in enumerate((up, down)):
            arrived(relay.at[n], r11.at[n])
            passed[n] = summed[near, halves[n]] + relay[n]
            give_half(n, passed.at[n], near)

    order = y_off + [0]
    for n, o in enumerate(order):
        q = (y + o) % ny
        first = 2 * q * share
        for s, value in enumerate(terms(last, first, 2 * share)):
            ended[q, s] = part[first + s] + value
        pending.append(
            send(ended.at[q, pl.ds((1 - core) * share, share)], got.at[q], s4.at[q], r4.at[q], partner)
        )
        if n:
            merge(order[n - 1])
    merge(0)
    pass_on()

    per = half // 8
    for v in range(2):
        for g in range(groups):
            image[pl.ds(2 * g + v, half, stride=2 * groups), :] = final[
                v * per : (v + 1) * per, g, 1
            ].reshape(half, 128)

    total = summed[y]
    for q in (down, up):
        for n in range(2):
            arrived(pieces.at[q, halves[n]], r5.at[q, n])
        total = total + pieces[q]
    grad[...] = total
    for copy in pending:
        copy.wait_send()


def write_out(image, grad, image_out, grad_out, sems):
    copies = [
        pltpu.make_async_copy(src, dst, sems.at[n])
        for n, (src, dst) in enumerate(((image, image_out), (grad, grad_out)))
    ]
    for copy in copies:
        copy.start()
    for copy in copies:
        copy.wait()


def on_device(nx, nz, ny, density, row_index, row_weight, col_index, col_weight, assignment, target_image):
    slices, cells = density.shape[0], density.shape[1]
    views, flat = target_image.shape
    pixels = row_index.shape[1]
    wide, tiles = 2 * pixels, flat * views // (8 * 2 * pixels)
    chunks = tiles // nz
    share = slices // (2 * ny)
    lines = flat // 128
    groups = wide // 128
    units = chunks - 1 + groups
    vm = pl.BlockSpec(memory_space=pltpu.VMEM)
    dma = pltpu.SemaphoreType.DMA
    image, grad = pl.pallas_call(
        functools.partial(kernel, (nx, nz, ny, slices * nx * nz)),
        out_shape=(
            jax.ShapeDtypeStruct((views * lines, 128), F32),
            jax.ShapeDtypeStruct((share, cells, cells), F32),
        ),
        in_specs=[pl.BlockSpec(memory_space=pltpu.HBM)] * 7,
        out_specs=(vm, vm),
        scratch_shapes=[
            pltpu.SMEM(assignment.shape, jnp.int32),
            pltpu.VMEM(density.shape, BF),
            pltpu.VMEM(row_index.shape, jnp.int32),
            pltpu.VMEM(row_index.shape, F32),
            pltpu.VMEM(row_index.shape, jnp.int32),
            pltpu.VMEM(row_index.shape, F32),
            pltpu.VMEM((views * lines, 128), F32),
            dma((7,)),
            pltpu.VMEM((8, wide), jnp.int32),
            pltpu.VMEM((8, wide), F32),
            pltpu.VMEM((2, 2 * cells, cells), F32),
            pltpu.VMEM((wide, cells), BF),
            pltpu.VMEM((chunks, cells, 16 * nz), BF),
            pltpu.VMEM((2, 2 * cells, wide), BF),
            pltpu.VMEM((2, wide, 2 * cells), BF),
            pltpu.VMEM((slices, 8 * nz, 2 * cells), BF),
            pltpu.VMEM((slices, pixels, wide), F32),
            pltpu.VMEM((pixels, wide), F32),
            pltpu.VMEM((pixels, wide), F32),
            pltpu.VMEM((pixels, wide), F32),
            pltpu.VMEM((tiles, groups, 2, 8, 128), F32),
            pltpu.VMEM((chunks, nz, groups, 2, 8, 128), F32),
            pltpu.VMEM((chunks, nz, groups, 8, 128), F32),
            pltpu.VMEM((chunks, groups, 2, 8, 128), F32),
            pltpu.VMEM((chunks, nx, groups, 2, 8, 128), F32),
            pltpu.VMEM((chunks, nz, groups, 2, 8, 128), F32),
            pltpu.VMEM((tiles, groups, 2, 8, 128), F32),
            pltpu.VMEM((slices, cells, cells), F32),
            pltpu.VMEM((ny, 2 * share, cells, cells), F32),
            pltpu.VMEM((ny, share, cells, cells), F32),
            pltpu.VMEM((ny, share, cells, cells), F32),
            pltpu.VMEM((ny, share, cells, cells), F32),
            pltpu.VMEM((2, share // 2, cells, cells), F32),
            pltpu.VMEM((2, share // 2, cells, cells), F32),
            pltpu.VMEM((cells // (2 * ny), cells), F32),
            pltpu.VMEM((nz, cells // (2 * ny), cells), F32),
            pltpu.VMEM((cells // (2 * ny), cells), F32),
            pltpu.VMEM((nx, cells // (2 * ny), cells), F32),
            pltpu.VMEM((2 * ny, cells // (2 * ny), cells), F32),
            pltpu.VMEM((pixels, wide), F32),
            dma((units, nz)), dma((units, nz)),
            dma((units, nx)), dma((units, nx)),
            dma((units, nz)), dma((units, nz)),
            dma((ny,)), dma((ny,)),
            dma((ny, 2)), dma((ny, 2)),
            dma((nz,)), dma((nz,)),
            dma((nx,)), dma((nx,)),
            dma((2 * ny,)), dma((2 * ny,)),
            dma((2,)), dma((2,)),
        ],
        compiler_params=pltpu.CompilerParams(
            collective_id=0, has_side_effects=True, vmem_limit_bytes=50331648
        ),
    )(*[pltpu.with_memory_space_constraint(a, pltpu.HBM) for a in (
        assignment, density, row_index, row_weight, col_index, col_weight,
        target_image.reshape(views, lines, 128).transpose(1, 0, 2).reshape(views * lines, 128),
    )])
    image, grad = pl.pallas_call(
        write_out,
        out_shape=(
            jax.ShapeDtypeStruct(image.shape, F32),
            jax.ShapeDtypeStruct(grad.shape, F32),
        ),
        in_specs=[vm, vm],
        out_specs=(pl.BlockSpec(memory_space=pltpu.HBM),) * 2,
        scratch_shapes=[dma((2,))],
        compiler_params=pltpu.CompilerParams(vmem_limit_bytes=1 << 20),
    )(image, grad)
    return image.reshape(lines, views, 128).transpose(1, 0, 2).reshape(views, flat), grad


def solution(mesh, nz=ZDEV):
    placed = (P("depth", None, None), P(), P(), P(), P(), P("views"), P("views", None))
    nx, ny = mesh.shape["depth"] // nz, mesh.shape["views"] // 2
    return jax.shard_map(
        functools.partial(on_device, nx, nz, ny),
        mesh=mesh,
        in_specs=placed,
        out_specs=(P("views", None), P(("depth", "views"), None, None)),
        check_vma=False,
    )
```

```python
import functools

import jax
import jax.numpy as jnp
from jax import lax
from jax.experimental import pallas as pl
from jax.experimental.pallas import tpu as pltpu
from jax.sharding import PartitionSpec as P

MESH = pl.DeviceIdType.MESH
ZDEV = 8
BF = jnp.bfloat16
F32 = jnp.float32
LOG2E = 1.4426950408889634


def spread_order(n):
    out = []
    for k in range(1, n // 2 + 1):
        for o in (k, n - k):
            if o not in out and 0 < o < n:
                out.append(o)
    return out


def kernel(
    dims, *refs
):
    (
    assign_h, density_h, row_index_h, row_weight_h, col_index_h, col_weight_h, target_h, image, grad,
    assign, density, row_index, row_weight, col_index, col_weight, target, loads,
    pad_i, pad_w, tall, rows_m, rows_t, cols_m, cols_t, crossed, work, goal, gain, shift,
    mine, theirs, local, slab, slabs, back, final, part, ended, got, summed, pieces, relay, passed,
    mass, masses, slab_mass, slab_masses, before, ahead,
    s1, r1, s2, r2, s3, r3, s4, r4, s5, r5, s8, r8, s9, r9, s10, r10, s11, r11,
    ) = refs
    nx, nz, ny, levels = dims
    step = 1.5 / levels
    slices, cells = density.shape[0], density.shape[1]
    half = row_index.shape[1] // 2
    pixels = 2 * half
    wide = 2 * pixels
    chunks = 2 * half // 8 // nz
    share = slices // (2 * ny)
    groups = wide // 128
    last = chunks - 1
    units = [(k, slice(0, groups)) for k in range(last)] + [(last, slice(0, groups))]
    depth, vw = lax.axis_index("depth"), lax.axis_index("views")
    x, z = depth // nz, depth % nz
    y, core = vw // 2, vw % 2

    def at_z(q):
        return (x * nz + q, vw)

    def at_x(q):
        return (q * nz + z, vw)

    def at_y(q):
        return (depth, q * 2 + core)

    partner = (depth, y * 2 + 1 - core)
    beside = spread_order(2 * ny)
    rows_held = cells // (2 * ny)
    z_off, x_off, y_off = (spread_order(n)[::-1] for n in (nz, nx, ny))

    fetch = [
        pltpu.make_async_copy(src, dst, loads.at[n])
        for n, (src, dst) in enumerate(
            [
                (assign_h, assign), (row_index_h, row_index), (row_weight_h, row_weight),
                (col_index_h, col_index), (col_weight_h, col_weight),
                (density_h, density), (target_h, target),
            ]
        )
    ]
    for copy in fetch:
        copy.start()

    barrier = pltpu.get_barrier_semaphore()
    for o in z_off:
        pl.semaphore_signal(barrier, inc=1, device_id=at_z((z + o) % nz), device_id_type=MESH)
    for o in x_off:
        pl.semaphore_signal(barrier, inc=1, device_id=at_x((x + o) % nx), device_id_type=MESH)
    for o in beside:
        pl.semaphore_signal(barrier, inc=1, device_id=(depth, (vw + o) % (2 * ny)), device_id_type=MESH)

    for copy in fetch[:5]:
        copy.wait()
    pad_i[...] = jnp.full(pad_i.shape, -2, jnp.int32)
    pad_w[...] = jnp.zeros(pad_w.shape, F32)
    for v in range(2):
        a = assign[v]
        pad_i[v : v + 1, 0:pixels] = row_index[pl.ds(a, 1), :]
        pad_w[v : v + 1, 0:pixels] = row_weight[pl.ds(a, 1), :]
        pad_i[2 + v : 3 + v, 0:pixels] = col_index[pl.ds(a, 1), :]
        pad_w[2 + v : 3 + v, 0:pixels] = col_weight[pl.ds(a, 1), :]

    def resampler(row, lanes):
        idx, w = pad_i[row : row + 1, 0:lanes], pad_w[row : row + 1, 0:lanes]
        places = lax.broadcasted_iota(jnp.int32, (cells, lanes), 0)
        zero = jnp.zeros((cells, lanes), F32)
        return jnp.where(places == idx, 1.0 - w, zero) + jnp.where(places == idx + 1, w, zero)

    tall_rows = 8 * nz

    def resamplers(v):
        tall[v] = resampler(v, 2 * cells).T
        for p in range(2):
            rows_m[p * pixels + v * half : p * pixels + (v + 1) * half, :] = tall[
                v, pl.ds(p, half, stride=2), :
            ].astype(BF)
        ct = resampler(2 + v, wide)
        cols_m[v] = jnp.concatenate([ct, pltpu.roll(ct, pixels, 1)], axis=0).astype(BF)

    def transposed():
        for v in range(2):
            cols_t[v] = cols_m[v].T
        for k in range(chunks):
            at = k * tall_rows
            rows_t[k] = jnp.concatenate(
                [rows_m[p * pixels + at : p * pixels + at + tall_rows, :] for p in range(2)], axis=0
            ).T

    def views_in(k):
        out = []
        for v in range(2):
            lo, hi = max(k * tall_rows, v * half), min((k + 1) * tall_rows, (v + 1) * half)
            if lo < hi:
                out.append((v, lo - k * tall_rows, hi - lo))
        return out

    def sample(k):
        at = k * tall_rows
        lhs = jnp.concatenate(
            [rows_m[p * pixels + at : p * pixels + at + tall_rows, :] for p in range(2)], axis=0
        )
        for pair in range(slices // 2):
            two = jnp.concatenate([density[2 * pair], density[2 * pair + 1]], axis=1)
            out = jnp.dot(lhs, two, preferred_element_type=F32).astype(BF)
            for s in range(2):
                cut = out[:, s * cells : (s + 1) * cells]
                crossed[2 * pair + s] = jnp.concatenate([cut[:tall_rows], cut[tall_rows:]], axis=1)
        for v, first, n in views_in(k):
            out = jnp.dot(
                crossed[:, first : first + n, :].reshape(slices * n, 2 * cells),
                cols_m[v],
                preferred_element_type=F32,
            )
            work[:, at + first : at + first + n, :] = out.reshape(slices, n, wide)

    def march(tile):
        at = pl.ds(pl.multiple_of(tile * 8, 8), 8)
        through = jnp.ones((8, wide), F32)
        inclusive = jnp.zeros((8, wide), F32)
        for s in range(slices):
            value = work[s, at, :]
            optical = step * value
            att = jnp.exp2(value * (-step * LOG2E))
            gone = 1.0 - att
            inclusive = inclusive + through * (optical * gone)
            work[s, at, :] = through * (gone + optical * att) + inclusive
            through = through * att
        for g in range(groups):
            lanes = slice(g * 128, (g + 1) * 128)
            mine[tile, g, 0] = inclusive[:, lanes] * (1.0 / step)
            mine[tile, g, 1] = through[:, lanes]

    pending = []

    def send(src, dst, ssem, rsem, device):
        copy = pltpu.make_async_remote_copy(
            src_ref=src, dst_ref=dst, send_sem=ssem, recv_sem=rsem, device_id=device, device_id_type=MESH
        )
        copy.start()
        return copy

    def arrived(dst, rsem):
        pltpu.make_async_remote_copy(
            src_ref=dst, dst_ref=dst, send_sem=rsem, recv_sem=rsem, device_id=partner, device_id_type=MESH
        ).wait_recv()

    def mass_sent():
        held = density[:, pl.ds(pl.multiple_of(vw * rows_held, rows_held), rows_held), :]
        one = jnp.sum(held.astype(F32), axis=0)
        mass[...] = one
        masses[z] = one
        for o in z_off:
            q = (z + o) % nz
            pending.append(send(mass, masses.at[z], s8.at[q], r8.at[z], at_z(q)))

    def mass_along_z():
        for o in z_off:
            q = (z + o) % nz
            arrived(masses.at[q], r8.at[q])
        lead = jnp.zeros((rows_held, cells), F32)
        total = lead
        for q in range(nz):
            lead = jnp.where(q == z, total, lead)
            total = total + masses[q]
        slab_mass[...] = total
        before[vw] = lead
        for o in x_off:
            q = (x + o) % nx
            pending.append(send(slab_mass, slab_masses.at[x], s9.at[q], r9.at[x], at_x(q)))

    def mass_along_x():
        slab_masses[x] = jnp.zeros((rows_held, cells), F32)
        for o in x_off:
            q = (x + o) % nx
            arrived(slab_masses.at[q], r9.at[q])
        lead = before[vw]
        for q in range(nx):
            lead = lead + jnp.where(q < x, slab_masses[q], 0.0)
        before[vw] = lead
        for o in beside:
            q = (vw + o) % (2 * ny)
            pending.append(send(before.at[vw], before.at[vw], s10.at[q], r10.at[vw], (depth, q)))

    def split(value):
        high = value.astype(BF)
        return high, (value - high.astype(F32)).astype(BF)

    def see_ahead():
        for o in beside:
            q = (vw + o) % (2 * ny)
            arrived(before.at[q], r10.at[q])
        two = jnp.concatenate(split(before[...].reshape(cells, cells)), axis=1)
        out = jnp.dot(rows_m[...], two, preferred_element_type=F32)
        out = out[:, :cells] + out[:, cells:]
        parts = split(jnp.concatenate([out[:pixels], out[pixels:]], axis=1))
        for v in range(2):
            at = slice(v * half, (v + 1) * half)
            passed = sum(jnp.dot(part[at], cols_m[v], preferred_element_type=F32) for part in parts)
            ahead[at] = jnp.exp2(passed * (-step * LOG2E))

    def send_share(u, q):
        k, gs = units[u]
        pending.append(
            send(mine.at[k * nz + q, gs], theirs.at[k, z, gs], s1.at[u, q], r1.at[u, z], at_z(q))
        )

    built = 0
    for k in range(chunks):
        for v, _, _ in views_in(k):
            if v >= built:
                resamplers(v)
                built = v + 1
        if k == 0:
            fetch[5].wait()
        sample(k)
        for q in range(nz):
            march(k * nz + q)
        if k == 0:
            pl.semaphore_wait(barrier, len(z_off) + len(x_off) + len(beside))
        for u in [k] if k < last else range(last, len(units)):
            for o in z_off:
                send_share(u, (z + o) % nz)
        if k == 0:
            mass_sent()
    transposed()

    fetch[6].wait()
    for v in range(2):
        for g in range(groups):
            goal[v * half : (v + 1) * half, g * 128 : (g + 1) * 128] = target[
                pl.ds(2 * g + v, half, stride=2 * groups), :
            ]

    def slab_of(u):
        k, gs = units[u]
        theirs[k, z, gs] = mine[k * nz + z, gs]
        for o in z_off:
            q = (z + o) % nz
            arrived(theirs.at[k, q, gs], r1.at[u, q])
        c = jnp.zeros((gs.stop - gs.start, 8, 128), F32)
        t = jnp.ones((gs.stop - gs.start, 8, 128), F32)
        for q in range(nz):
            local[k, q, gs] = c
            c = c + t * theirs[k, q, gs, 0]
            t = t * theirs[k, q, gs, 1]
        slab[k, gs, 0] = c
        slab[k, gs, 1] = t
        slabs[k, x, gs, 0] = c
        slabs[k, x, gs, 1] = t
        for o in x_off:
            q = (x + o) % nx
            pending.append(send(slab.at[k, gs], slabs.at[k, x, gs], s2.at[u, q], r2.at[u, x], at_x(q)))

    def lead_of(u):
        k, gs = units[u]
        for o in x_off:
            q = (x + o) % nx
            arrived(slabs.at[k, q, gs], r2.at[u, q])
        lead_c = jnp.zeros((gs.stop - gs.start, 8, 128), F32)
        lead_t = jnp.ones((gs.stop - gs.start, 8, 128), F32)
        c, t = lead_c, lead_t
        for q in range(nx):
            c = c + t * slabs[k, q, gs, 0]
            t = t * slabs[k, q, gs, 1]
            earlier = q < x
            lead_c = jnp.where(earlier, c, lead_c)
            lead_t = jnp.where(earlier, t, lead_t)
        own = k * nz + z
        for q in range(nz):
            back[k, q, gs, 0] = c - (lead_c + lead_t * local[k, q, gs])
            back[k, q, gs, 1] = c
        for o in z_off:
            q = (z + o) % nz
            pending.append(send(back.at[k, q, gs], final.at[own, gs], s3.at[u, q], r3.at[u, z], at_z(q)))
        final[own, gs] = back[k, z, gs]

    def weigh(k):
        for u, (j, gs) in enumerate(units):
            if j == k:
                for o in z_off:
                    q = (z + o) % nz
                    arrived(final.at[k * nz + q, gs], r3.at[u, q])
        at = slice(k * tall_rows, (k + 1) * tall_rows)
        tiles = slice(k * nz, (k + 1) * nz)
        total = jnp.concatenate([final[tiles, g, 1].reshape(tall_rows, 128) for g in range(groups)], axis=1)
        residue = levels * (total - goal[at])
        gain[at] = residue * ahead[at]
        behind = jnp.concatenate([final[tiles, g, 0].reshape(tall_rows, 128) for g in range(groups)], axis=1)
        shift[at] = step * residue * behind

    def terms(k, first, count):
        at = slice(k * tall_rows, (k + 1) * tall_rows)
        g = [(gain[at] * work[first + s, at] - shift[at]).astype(BF) for s in range(count)]
        spread = [
            (
                n,
                jnp.dot(
                    jnp.concatenate([g[s][a : a + n] for s in range(count)], axis=0),
                    cols_t[v],
                    preferred_element_type=F32,
                ).astype(BF),
            )
            for v, a, n in views_in(k)
        ]
        out = []
        for pair in range(0, count, 2):
            stack = jnp.concatenate(
                [
                    jnp.concatenate(
                        [
                            value[s * n : (s + 1) * n, p * cells : (p + 1) * cells]
                            for p in range(2)
                            for n, value in spread
                        ],
                        axis=0,
                    )
                    for s in (pair, pair + 1)
                ],
                axis=1,
            )
            both = jnp.dot(rows_t[k], stack, preferred_element_type=F32)
            out += [both[:, :cells], both[:, cells:]]
        return out

    def collect(k):
        def body(i, carry):
            for s, value in enumerate(terms(k, 4 * i, 4)):
                part[4 * i + s] = value if k == 0 else part[4 * i + s] + value
            return carry

        lax.fori_loop(0, slices // 4, body, 0)

    slab_of(0)
    mass_along_z()
    lead_of(0)
    mass_along_x()
    for k in range(1, last):
        slab_of(k)
        if k == last - 1:
            slab_of(last)
        lead_of(k)
    see_ahead()
    for u in range(last + 1, len(units)):
        slab_of(u)
    for u in range(last, len(units)):
        lead_of(u)
    for k in range(last):
        weigh(k)
        collect(k)
    weigh(last)

    up, down = (y + 1) % ny, (y + ny - 1) % ny
    halves = slice(0, share // 2), slice(share // 2, share)

    def give_half(n, src, q):
        pending.append(send(src, pieces.at[y, halves[n]], s5.at[q, n], r5.at[y, n], at_y(q)))

    def merge(o):
        q = (y + o) % ny
        arrived(got.at[q], r4.at[q])
        summed[q] = ended[q, pl.ds(core * share, share)] + got[q]
        if o == 2:
            for n, near in enumerate((up, down)):
                pending.append(send(summed.at[q, halves[n]], relay.at[n], s11.at[n], r11.at[n], at_y(near)))
        elif o == 1:
            give_half(1, summed.at[q, halves[1]], q)
        elif o == 3:
            give_half(0, summed.at[q, halves[0]], q)

    def pass_on():
        for n, near in enumerate((up, down)):
            arrived(relay.at[n], r11.at[n])
            passed[n] = summed[near, halves[n]] + relay[n]
            give_half(n, passed.at[n], near)

    order = y_off + [0]
    for n, o in enumerate(order):
        q = (y + o) % ny
        first = 2 * q * share
        for s, value in enumerate(terms(last, first, 2 * share)):
            ended[q, s] = part[first + s] + value
        pending.append(
            send(ended.at[q, pl.ds((1 - core) * share, share)], got.at[q], s4.at[q], r4.at[q], partner)
        )
        if n:
            merge(order[n - 1])
    merge(0)
    pass_on()

    per = half // 8
    for v in range(2):
        for g in range(groups):
            image[pl.ds(2 * g + v, half, stride=2 * groups), :] = final[
                v * per : (v + 1) * per, g, 1
            ].reshape(half, 128)

    total = summed[y]
    for q in (down, up):
        for n in range(2):
            arrived(pieces.at[q, halves[n]], r5.at[q, n])
        total = total + pieces[q]
    grad[...] = total
    for copy in pending:
        copy.wait_send()


def write_out(image, grad, image_out, grad_out, sems):
    copies = [
        pltpu.make_async_copy(src, dst, sems.at[n])
        for n, (src, dst) in enumerate(((image, image_out), (grad, grad_out)))
    ]
    for copy in copies:
        copy.start()
    for copy in copies:
        copy.wait()


def on_device(nx, nz, ny, density, row_index, row_weight, col_index, col_weight, assignment, target_image):
    slices, cells = density.shape[0], density.shape[1]
    views, flat = target_image.shape
    pixels = row_index.shape[1]
    wide, tiles = 2 * pixels, flat * views // (8 * 2 * pixels)
    chunks = tiles // nz
    share = slices // (2 * ny)
    lines = flat // 128
    groups = wide // 128
    units = chunks - 1 + groups
    vm = pl.BlockSpec(memory_space=pltpu.VMEM)
    dma = pltpu.SemaphoreType.DMA
    image, grad = pl.pallas_call(
        functools.partial(kernel, (nx, nz, ny, slices * nx * nz)),
        out_shape=(
            jax.ShapeDtypeStruct((views * lines, 128), F32),
            jax.ShapeDtypeStruct((share, cells, cells), F32),
        ),
        in_specs=[pl.BlockSpec(memory_space=pltpu.HBM)] * 7,
        out_specs=(vm, vm),
        scratch_shapes=[
            pltpu.SMEM(assignment.shape, jnp.int32),
            pltpu.VMEM(density.shape, BF),
            pltpu.VMEM(row_index.shape, jnp.int32),
            pltpu.VMEM(row_index.shape, F32),
            pltpu.VMEM(row_index.shape, jnp.int32),
            pltpu.VMEM(row_index.shape, F32),
            pltpu.VMEM((views * lines, 128), F32),
            dma((7,)),
            pltpu.VMEM((8, wide), jnp.int32),
            pltpu.VMEM((8, wide), F32),
            pltpu.VMEM((2, 2 * cells, cells), F32),
            pltpu.VMEM((wide, cells), BF),
            pltpu.VMEM((chunks, cells, 16 * nz), BF),
            pltpu.VMEM((2, 2 * cells, wide), BF),
            pltpu.VMEM((2, wide, 2 * cells), BF),
            pltpu.VMEM((slices, 8 * nz, 2 * cells), BF),
            pltpu.VMEM((slices, pixels, wide), F32),
            pltpu.VMEM((pixels, wide), F32),
            pltpu.VMEM((pixels, wide), F32),
            pltpu.VMEM((pixels, wide), F32),
            pltpu.VMEM((tiles, groups, 2, 8, 128), F32),
            pltpu.VMEM((chunks, nz, groups, 2, 8, 128), F32),
            pltpu.VMEM((chunks, nz, groups, 8, 128), F32),
            pltpu.VMEM((chunks, groups, 2, 8, 128), F32),
            pltpu.VMEM((chunks, nx, groups, 2, 8, 128), F32),
            pltpu.VMEM((chunks, nz, groups, 2, 8, 128), F32),
            pltpu.VMEM((tiles, groups, 2, 8, 128), F32),
            pltpu.VMEM((slices, cells, cells), F32),
            pltpu.VMEM((ny, 2 * share, cells, cells), F32),
            pltpu.VMEM((ny, share, cells, cells), F32),
            pltpu.VMEM((ny, share, cells, cells), F32),
            pltpu.VMEM((ny, share, cells, cells), F32),
            pltpu.VMEM((2, share // 2, cells, cells), F32),
            pltpu.VMEM((2, share // 2, cells, cells), F32),
            pltpu.VMEM((cells // (2 * ny), cells), F32),
            pltpu.VMEM((nz, cells // (2 * ny), cells), F32),
            pltpu.VMEM((cells // (2 * ny), cells), F32),
            pltpu.VMEM((nx, cells // (2 * ny), cells), F32),
            pltpu.VMEM((2 * ny, cells // (2 * ny), cells), F32),
            pltpu.VMEM((pixels, wide), F32),
            dma((units, nz)), dma((units, nz)),
            dma((units, nx)), dma((units, nx)),
            dma((units, nz)), dma((units, nz)),
            dma((ny,)), dma((ny,)),
            dma((ny, 2)), dma((ny, 2)),
            dma((nz,)), dma((nz,)),
            dma((nx,)), dma((nx,)),
            dma((2 * ny,)), dma((2 * ny,)),
            dma((2,)), dma((2,)),
        ],
        compiler_params=pltpu.CompilerParams(
            collective_id=0, has_side_effects=True, vmem_limit_bytes=50331648
        ),
    )(*[pltpu.with_memory_space_constraint(a, pltpu.HBM) for a in (
        assignment, density, row_index, row_weight, col_index, col_weight,
        target_image.reshape(views, lines, 128).transpose(1, 0, 2).reshape(views * lines, 128),
    )])
    image, grad = pl.pallas_call(
        write_out,
        out_shape=(
            jax.ShapeDtypeStruct(image.shape, F32),
            jax.ShapeDtypeStruct(grad.shape, F32),
        ),
        in_specs=[vm, vm],
        out_specs=(pl.BlockSpec(memory_space=pltpu.HBM),) * 2,
        scratch_shapes=[dma((2,))],
        compiler_params=pltpu.CompilerParams(vmem_limit_bytes=1 << 20),
    )(image, grad)
    return image.reshape(lines, views, 128).transpose(1, 0, 2).reshape(views, flat), grad


def solution(mesh, nz=ZDEV):
    placed = (P("depth", None, None), P(), P(), P(), P(), P("views"), P("views", None))
    nx, ny = mesh.shape["depth"] // nz, mesh.shape["views"] // 2
    return jax.shard_map(
        functools.partial(on_device, nx, nz, ny),
        mesh=mesh,
        in_specs=placed,
        out_specs=(P("views", None), P(("depth", "views"), None, None)),
        check_vma=False,
    )
```
